512 devices in a mesh: cells: 128 (over y, z, core), env: 4 (over x).
Axes of the slice: x: 4, y: 8, z: 8, core: 2. Of those that a mesh axis runs over, the one named last changes fastest.
Arguments:
- archive: bfloat16 [256, 1048576], P('cells', 'env'), may hold values from -6 to 6
- fitness_old: float32 [256], P('cells'), may hold values from -30 to -0.3
- parents: int32 [128], replicated, may hold values from 0 to 255, as said below
- cell_ids: int32 [128], replicated, may hold values from 0 to 255
- replace_mask: int32 [128], replicated, may hold values 0 or 1
- noise: bfloat16 [128, 1048576], P('cells', 'env'), may hold values from -1.796875 to 1.796875
- start_states: float32 [256, 512], P('env'), may hold values from -6 to 6
- forces: bfloat16 [16, 256, 128], P(None, 'env')
- dyn_blocks: bfloat16 [4, 128, 128], replicated
- act_map: bfloat16 [512, 512], replicated, may hold values from -0.25 to 0.25
- contact_map: bfloat16 [128, 512], replicated, may hold values from -0.5 to 0.5
- cost_weights: float32 [512], replicated, may hold values from 0.2 to 2
Outputs:
- new_archive: bfloat16 [256, 1048576], P('cells', 'env')
- new_fitness: float32 [256], P('cells')
- cell_gain: float32 [256], P('cells')
The draws below stay inside these ranges and needn't reach their ends.
Inputs may be any that keep to these rules, and one draw needn't show every extreme that they name: Of the 2 cells i * 2 to (i+1) * 2 - 1, at most 1 distinct ones are parents, for every i.
All inputs are finite; a program needn't handle non-finite values.
Results may differ from the reference program's by a relative error of at most 0.0004.
Values may be sent and summed in bfloat16 or wider, within the bound.
A program may use at most 64 MiB of HBM per device.

```python
import math
import jax
import jax.numpy as jnp
import numpy as np
from jax import lax

NS = 512
HID = 1024
ACT = 512
BLK = 128
NC = 128
STEPS = 16
CELL_DEV = 2
USED_DEV = 1
PARAMS = 1048576
CELLS = 256
OFFSPRING = 128
ENVS = 256
N_CELLS = 128


def draw_fitness_old(key, part):
    spread = jax.random.uniform(key, (CELLS,), jnp.float32, -1.2039728, 3.4011974)
    return -jnp.exp(spread)


def draw_parents(key, part):
    key_offset, key_rank, key_left, key_right, key_slot = jax.random.split(key, 5)
    offsets = jax.random.randint(key_offset, (N_CELLS,), 0, CELL_DEV - USED_DEV + 1)
    offsets = offsets.at[0].set(0).at[N_CELLS - 1].set(CELL_DEV - USED_DEV)
    ranking = jax.random.permutation(key_rank, N_CELLS)
    draw_left = jax.random.randint(key_left, (OFFSPRING,), 0, N_CELLS)
    draw_right = jax.random.randint(key_right, (OFFSPRING,), 0, N_CELLS)
    device = jnp.take(ranking, draw_left * draw_right // N_CELLS)
    slot_pick = jax.random.randint(key_slot, (OFFSPRING,), 0, USED_DEV)
    counter = jnp.arange(OFFSPRING, dtype=jnp.int32)
    leading = (counter >= 2) & (counter < 2 + USED_DEV)
    device = jnp.where(leading, ranking[0], device)
    slot_pick = jnp.where(leading, (counter - 2) % USED_DEV, slot_pick)
    device = jnp.where(counter == 0, N_CELLS - 1, device)
    slot_pick = jnp.where(counter == 0, USED_DEV - 1, slot_pick)
    device = jnp.where(counter == 1, 0, device)
    slot_pick = jnp.where(counter == 1, 0, slot_pick)
    return (device * CELL_DEV + jnp.take(offsets, device) + slot_pick).astype(jnp.int32)


def draw_forces(key, part):
    rows = jnp.arange(ENVS, dtype=jnp.float32)
    ramp = 0.6 + 1.2 * rows / ENVS
    values = jax.random.normal(key, (STEPS, ENVS, NC), jnp.float32)
    return (values * ramp[None, :, None]).astype(jnp.bfloat16)


def draw_dyn_blocks(key, part):
    identity = jnp.eye(BLK, dtype=jnp.float32)[None, :, :]
    spread = jax.random.normal(key, (NS // BLK, BLK, BLK), jnp.float32)
    return (0.6 * identity + spread * (0.25 / BLK ** 0.5)).astype(jnp.bfloat16)


def plant(entries, rng, least, top_value):
    longest = entries.shape.index(max(entries.shape))
    spots = []
    for shift in (0, 1):
        where = [jax.random.randint(jax.random.fold_in(rng, axis), (), 0, length) for axis, length in enumerate(entries.shape)]
        where[longest] = (where[longest] + shift) % entries.shape[longest]
        spots.append(tuple(where))
    return entries.at[spots[0]].set(least).at[spots[1]].set(top_value)


def block_levels(key, dims, cuts, smallest, top_value):
    factor_of = 1.0
    for dim, blocks in cuts:
        steps = jax.random.uniform(jax.random.fold_in(jax.random.fold_in(key, 6), dim), (blocks,), jnp.float32, smallest / len(cuts), top_value / len(cuts))
        factor_of = factor_of * jnp.repeat(jnp.exp(steps), dims[dim] // blocks).reshape((-1,) + (1,) * (len(dims) - 1 - dim))
    return factor_of


def rank_table(amount, lean):
    weights = [(1 << 20) // math.isqrt(grade ** lean) + 1 for grade in range(1, amount + 1)]
    width = 1 + sum(weights) // (1 << 30)
    return np.cumsum(np.array([max(1, weight // width) for weight in weights]))


def ranked(own_key, extent, amount, lean):
    listing = rank_table(amount, lean)
    pick = jax.random.randint(jax.random.fold_in(own_key, 1), extent, 0, int(listing[amount - 1]))
    standing = jnp.searchsorted(jnp.asarray(listing, jnp.int32), pick, side="right")
    return jax.random.permutation(jax.random.fold_in(own_key, 2), amount)[standing].astype(jnp.int32)


def centred(rng, dims, deviation, limit, cuts=(), kind=jnp.bfloat16):
    values = deviation * jax.random.normal(rng, dims, jnp.float32)
    if cuts:
        values = values * block_levels(rng, dims, cuts, -0.22, 0.18)
    return jnp.clip(values, -limit, limit).astype(kind)


def setup_inputs(seed: int = 0) -> dict:
    key_list = jax.random.split(jax.random.key(seed), 13)
    archive = centred(key_list[0], (CELLS, PARAMS), 1.0, 6.0, ((0, 128), (1, 4)))
    fitness_old = draw_fitness_old(jax.random.fold_in(key_list[12], 71), 0)
    parents = draw_parents(jax.random.fold_in(key_list[12], 71), 0)
    cell_ids = plant(ranked(key_list[3], (OFFSPRING,), CELLS, 2), jax.random.fold_in(key_list[3], 3), 0, CELLS - 1).astype(jnp.int32)
    replace_mask = plant((jax.random.randint(key_list[4], (OFFSPRING,), 0, 2) < 1).astype(jnp.int32), jax.random.fold_in(key_list[4], 1), 0, 1)
    noise = centred(key_list[5], (OFFSPRING, PARAMS), 0.3, 1.796875, ((0, 128), (1, 4)))
    start_states = centred(key_list[6], (ENVS, NS), 1.0, 6.0, ((0, 4),), jnp.float32)
    forces = draw_forces(jax.random.fold_in(key_list[12], 71), 0)
    dyn_blocks = draw_dyn_blocks(jax.random.fold_in(key_list[12], 71), 0)
    act_map = centred(key_list[9], (ACT, NS), ACT ** -0.5, 0.25)
    contact_map = centred(key_list[10], (NC, NS), NC ** -0.5, 0.5)
    cost_weights = jnp.clip(jnp.exp(jax.random.uniform(key_list[11], (NS,), jnp.float32, math.log(0.2), math.log(2.0))), 0.2, 2.0)
    return dict(archive=archive, fitness_old=fitness_old, parents=parents, cell_ids=cell_ids, replace_mask=replace_mask, noise=noise, start_states=start_states, forces=forces, dyn_blocks=dyn_blocks, act_map=act_map, contact_map=contact_map, cost_weights=cost_weights)


def roll_member(child, start_states, forces, dyn_blocks, act_map, contact_map, cost_weights):
    weight_in = child[:NS * HID].reshape(NS, HID)
    weight_out = child[NS * HID:].reshape(HID, ACT)
    envs = start_states.shape[0]

    def advance(carry, force_now):
        states, cost_sum = carry
        state_low = states.astype(jnp.bfloat16)
        hidden = jnp.tanh(jnp.dot(state_low, weight_in, preferred_element_type=jnp.float32) * (NS ** -0.5)).astype(jnp.bfloat16)
        action = (jnp.dot(hidden, weight_out, preferred_element_type=jnp.float32) * (HID ** -0.5)).astype(jnp.bfloat16)
        blocked = state_low.reshape(envs, NS // BLK, BLK).astype(jnp.float32)
        drifted = jnp.einsum("ebk,bkl->ebl", blocked, dyn_blocks.astype(jnp.float32)).reshape(envs, NS)
        states = drifted + jnp.dot(action, act_map, preferred_element_type=jnp.float32) + jnp.dot(force_now, contact_map, preferred_element_type=jnp.float32)
        cost_sum = cost_sum + jnp.sum(states * states * cost_weights)
        return (states, cost_sum), None

    (final_state, cost_sum), nothing = lax.scan(advance, (start_states, jnp.zeros((), jnp.float32)), forces)
    return cost_sum


def reference(archive, fitness_old, parents, cell_ids, replace_mask, noise, start_states, forces, dyn_blocks, act_map, contact_map, cost_weights):
    parent_rows = jnp.take(archive, parents, axis=0)
    children = (parent_rows.astype(jnp.float32) + noise.astype(jnp.float32)).astype(jnp.bfloat16)

    def evaluate(child):
        return roll_member(child, start_states, forces, dyn_blocks, act_map, contact_map, cost_weights)

    cost_sums = lax.map(evaluate, children)
    fitness = -cost_sums / (STEPS * ENVS * NS)
    cell_range = jnp.arange(CELLS, dtype=jnp.int32)
    matches = cell_ids[None, :] == cell_range[:, None]
    eligible = matches & (replace_mask[None, :] == 1)
    indices = jnp.arange(OFFSPRING, dtype=jnp.int32)
    winner = jnp.max(jnp.where(eligible, indices[None, :], -1), axis=1)
    chosen = winner >= 0
    safe_index = jnp.maximum(winner, 0).astype(jnp.int32)
    new_archive = jnp.where(chosen[:, None], jnp.take(children, safe_index, axis=0), archive)
    new_fitness = jnp.where(chosen, jnp.take(fitness, safe_index), fitness_old)
    lifted = jnp.maximum(fitness[None, :] - fitness_old[:, None], 0.0)
    cell_gain = jnp.sum(jnp.where(matches, lifted, 0.0), axis=1)
    return new_archive, new_fitness, cell_gain
```

```python
import functools

import jax
import jax.numpy as jnp
from jax import lax
from jax.experimental import pallas as pl
from jax.experimental.pallas import tpu as pltpu
from jax.sharding import Mesh
from jax.sharding import PartitionSpec as P

NS = 512
HID = 1024
ACT = 512
BLK = 128
STEPS = 16
CELLS = ("cells_0", "cells_1", "cells_2")
LANES = 128
SUB = 16
VMEM = pltpu.MemorySpace.VMEM
SMEM = pltpu.MemorySpace.SMEM


def pick_body(index_ref, rows_ref, out_ref):
    def one(k, carry):
        out_ref[k] = rows_ref[index_ref[k]]
        return carry

    lax.fori_loop(0, out_ref.shape[0], one, 0, unroll=8)


def pick_tiles(index, rows):
    count = index.shape[0]
    return pl.pallas_call(
        pick_body,
        out_shape=jax.ShapeDtypeStruct((count, *rows.shape[1:]), rows.dtype),
        in_specs=[pl.BlockSpec(memory_space=SMEM), pl.BlockSpec(memory_space=VMEM)],
        out_specs=pl.BlockSpec(memory_space=VMEM),
        name="pick_tiles",
    )(index, rows)


def rollout_body(
    weights_ref, start_ref, pushed_ref, dyn_ref, act_ref, cost_ref, out_ref, wide, w_in, w_out, mix
):
    half = weights_ref.shape[0] // 2
    wide[...] = weights_ref[:half].reshape(wide.shape).astype(jnp.float32)
    for j in range(HID // LANES):
        w_in[:, j * LANES : (j + 1) * LANES] = wide[
            pl.ds(j, NS, stride=HID // LANES), :
        ].astype(jnp.bfloat16)
    wide[...] = weights_ref[half:].reshape(wide.shape).astype(jnp.float32)
    for j in range(ACT // LANES):
        w_out[:, j * LANES : (j + 1) * LANES] = wide[
            pl.ds(j, HID, stride=ACT // LANES), :
        ].astype(jnp.bfloat16)
    mix[...] = (
        jnp.dot(w_out[...], act_ref[...], preferred_element_type=jnp.float32) * HID ** (-0.5)
    ).astype(jnp.bfloat16)
    envs = start_ref.shape[0]
    side = NS // 2

    def advance(t, carry):
        states, total = carry
        low = states.astype(jnp.bfloat16)
        hidden = jnp.tanh(
            jnp.dot(low, w_in[...], preferred_element_type=jnp.float32) * NS ** (-0.5)
        ).astype(jnp.bfloat16)
        drifted = jnp.concatenate(
            [
                jnp.dot(
                    low[:, n * side : (n + 1) * side],
                    dyn_ref[n],
                    preferred_element_type=jnp.float32,
                )
                for n in range(2)
            ],
            axis=1,
        )
        states = (
            drifted
            + jnp.dot(hidden, mix[...], preferred_element_type=jnp.float32)
            + pushed_ref[t]
        )
        squares = (states * states).reshape(envs // 8, 8, NS)
        return states, total + jnp.sum(squares, axis=0)

    last, total = lax.fori_loop(
        0, STEPS, advance, (start_ref[...], jnp.zeros((8, NS), jnp.float32))
    )
    weighted = total * cost_ref[...]
    out_ref[...] = jnp.full((8, LANES), jnp.sum(weighted), jnp.float32)


def rollout(weights, start_states, pushed, dyn_pairs, act_map, cost_weights):
    return pl.pallas_call(
        rollout_body,
        out_shape=jax.ShapeDtypeStruct((8, LANES), jnp.float32),
        in_specs=[pl.BlockSpec(memory_space=VMEM)] * 6,
        out_specs=pl.BlockSpec(memory_space=VMEM),
        scratch_shapes=[
            pltpu.VMEM((NS * HID // LANES, LANES), jnp.float32),
            pltpu.VMEM((NS, HID), jnp.bfloat16),
            pltpu.VMEM((HID, ACT), jnp.bfloat16),
            pltpu.VMEM((HID, NS), jnp.bfloat16),
        ],
        compiler_params=pltpu.CompilerParams(vmem_limit_bytes=40 * 1024 * 1024),
        cost_estimate=pl.CostEstimate(
            flops=STEPS * 2 * 64 * NS * 2 * HID * 8, bytes_accessed=8 << 20, transcendentals=1 << 20
        ),
        name="rollout",
    )(weights, start_states, pushed, dyn_pairs, act_map, cost_weights)


PHASES = (("cells_2", "env"), ("cells_1",), ("cells_0",))


def phase_peers(phase, sizes):
    axes = PHASES[phase]
    offsets = [{}]
    for axis in axes:
        offsets = [{**o, axis: d} for o in offsets for d in range(sizes[axis])]
    peers = []
    for offset in offsets[1:]:
        peers.append(
            {a: lax.rem(lax.axis_index(a) + d, sizes[a]) for a, d in offset.items()}
        )
    return peers


def sum_body(sizes, value_ref, out_ref, sums, landed, send_sem, recv_sem):
    everyone = [phase_peers(phase, sizes) for phase in range(len(PHASES))]
    barrier = pltpu.get_barrier_semaphore()
    for peers in everyone:
        for peer in peers:
            pl.semaphore_signal(
                barrier, inc=1, device_id=peer, device_id_type=pl.DeviceIdType.MESH
            )
    pl.semaphore_wait(barrier, sum(len(peers) for peers in everyone))
    sums[0] = value_ref[...]
    for phase, peers in enumerate(everyone):
        copies = []
        for d, peer in enumerate(peers):
            copy = pltpu.make_async_remote_copy(
                src_ref=sums.at[phase],
                dst_ref=landed.at[phase, d],
                send_sem=send_sem.at[phase, d],
                recv_sem=recv_sem.at[phase, d],
                device_id=peer,
                device_id_type=pl.DeviceIdType.MESH,
            )
            copy.start()
            copies.append(copy)
        for copy in copies:
            copy.wait()
        total = sums[phase]
        for d in range(len(peers)):
            total = total + landed[phase, d]
        if phase + 1 < len(PHASES):
            sums[phase + 1] = total
        else:
            out_ref[...] = total


def sum_over_all(value, sizes):
    most = 7
    return pl.pallas_call(
        functools.partial(sum_body, sizes),
        out_shape=jax.ShapeDtypeStruct(value.shape, value.dtype),
        in_specs=[pl.BlockSpec(memory_space=VMEM)],
        out_specs=pl.BlockSpec(memory_space=VMEM),
        scratch_shapes=[
            pltpu.VMEM((len(PHASES), *value.shape), value.dtype),
            pltpu.VMEM((len(PHASES), most, *value.shape), value.dtype),
            pltpu.SemaphoreType.DMA((len(PHASES), most)),
            pltpu.SemaphoreType.DMA((len(PHASES), most)),
        ],
        compiler_params=pltpu.CompilerParams(collective_id=0, has_side_effects=True),
        name="sum_over_all",
    )(value)


def on_device(
    sizes,
    archive,
    fitness_old,
    parents,
    cell_ids,
    replace_mask,
    noise,
    start_states,
    forces,
    dyn_blocks,
    act_map,
    contact_map,
    cost_weights,
):
    cell_dev = archive.shape[0]
    cell_count = lax.axis_size(CELLS)
    total_cells = cell_dev * cell_count
    offspring_count = parents.shape[0]
    position = lax.axis_index(CELLS)
    tiled = (cell_count, SUB, LANES)

    used_first = jnp.any(parents == position * cell_dev)
    compact = jnp.where(used_first, archive[0], archive[1]).reshape(tiled)
    columns = lax.all_to_all(compact, CELLS, split_axis=0, concat_axis=0, tiled=True)
    parent_cols = pick_tiles(parents // cell_dev, columns)
    parent_rows = lax.all_to_all(parent_cols, CELLS, split_axis=0, concat_axis=0, tiled=True)
    noise_tiles = noise[0].reshape(tiled)
    children = (parent_rows.astype(jnp.float32) + noise_tiles.astype(jnp.float32)).astype(
        jnp.bfloat16
    )

    cell_range = jnp.arange(total_cells, dtype=jnp.int32)
    matches = cell_ids[None, :] == cell_range[:, None]
    eligible = matches & (replace_mask[None, :] == 1)
    indices = jnp.arange(offspring_count, dtype=jnp.int32)
    winner = jnp.max(jnp.where(eligible, indices[None, :], -1), axis=1)
    winning = indices[None, :] == winner[:, None]
    chosen = winner >= 0

    copies = jnp.broadcast_to(children, (lax.axis_size("env"), *tiled))
    weights = lax.all_to_all(copies, "env", split_axis=0, concat_axis=0, tiled=True)

    child_cols = lax.all_to_all(children, CELLS, split_axis=0, concat_axis=0, tiled=True)
    placed = jnp.dot(
        winning.astype(jnp.bfloat16),
        child_cols.reshape(cell_count, SUB * LANES),
        preferred_element_type=jnp.float32,
    ).astype(jnp.bfloat16)
    replaced = lax.all_to_all(
        placed.reshape(cell_count, cell_dev, SUB * LANES),
        CELLS,
        split_axis=0,
        concat_axis=0,
        tiled=True,
    )
    replaced = jnp.moveaxis(replaced, 1, 0).reshape(archive.shape)
    own_chosen = lax.dynamic_slice_in_dim(chosen, position * cell_dev, cell_dev, 0)
    new_archive = jnp.where(own_chosen[:, None], replaced, archive)

    envs = start_states.shape[0]
    pushed = jnp.dot(
        forces.reshape(STEPS * envs, -1), contact_map, preferred_element_type=jnp.float32
    ).reshape(STEPS, envs, NS)
    dyn_pairs = (
        dyn_blocks.reshape(2, 2, BLK, 1, BLK)
        * jnp.eye(2, dtype=jnp.bfloat16)[None, :, None, :, None]
    ).reshape(2, 2 * BLK, 2 * BLK)
    cost = rollout(
        weights, start_states, pushed, dyn_pairs, act_map, cost_weights.reshape(1, NS)
    )
    slots = jnp.where(indices[None, :] == position, cost, 0.0)
    all_costs = sum_over_all(slots, sizes)[0]

    envs_total = envs * lax.axis_size("env")
    fitness = -all_costs / (STEPS * envs_total * NS)
    own_winning = lax.dynamic_slice_in_dim(winning, position * cell_dev, cell_dev, 0)
    own_matches = lax.dynamic_slice_in_dim(matches, position * cell_dev, cell_dev, 0)
    winner_fitness = jnp.sum(jnp.where(own_winning, fitness[None, :], 0.0), axis=1)
    new_fitness = jnp.where(own_chosen, winner_fitness, fitness_old)
    lifted = jnp.maximum(fitness[None, :] - fitness_old[:, None], 0.0)
    cell_gain = jnp.sum(jnp.where(own_matches, lifted, 0.0), axis=1)
    return (new_archive, new_fitness, cell_gain)


def solution(mesh):
    split = Mesh(
        mesh.devices.reshape(8, 8, 2, mesh.shape["env"]), ("cells_0", "cells_1", "cells_2", "env")
    )
    return jax.shard_map(
        functools.partial(on_device, dict(split.shape)),
        mesh=split,
        in_specs=(
            P(CELLS, "env"),
            P(CELLS),
            P(),
            P(),
            P(),
            P(CELLS, "env"),
            P("env", None),
            P(None, "env", None),
            P(),
            P(),
            P(),
            P(),
        ),
        out_specs=(P(CELLS, "env"), P(CELLS), P(CELLS)),
        check_vma=False,
    )
```

```python
import functools

import jax
import jax.numpy as jnp
from jax import lax
from jax.experimental import pallas as pl
from jax.experimental.pallas import tpu as pltpu
from jax.sharding import Mesh
from jax.sharding import PartitionSpec as P

NS = 512
HID = 1024
ACT = 512
BLK = 128
STEPS = 16
CELLS = ("cells_0", "cells_1", "cells_2")
LANES = 128
SUB = 16
VMEM = pltpu.MemorySpace.VMEM
SMEM = pltpu.MemorySpace.SMEM


def pick_body(index_ref, rows_ref, out_ref):
    def one(k, carry):
        out_ref[k] = rows_ref[index_ref[k]]
        return carry

    lax.fori_loop(0, out_ref.shape[0], one, 0, unroll=8)


def pick_tiles(index, rows):
    count = index.shape[0]
    return pl.pallas_call(
        pick_body,
        out_shape=jax.ShapeDtypeStruct((count, *rows.shape[1:]), rows.dtype),
        in_specs=[pl.BlockSpec(memory_space=SMEM), pl.BlockSpec(memory_space=VMEM)],
        out_specs=pl.BlockSpec(memory_space=VMEM),
        name="pick_tiles",
    )(index, rows)


def rollout_body(
    weights_ref, start_ref, pushed_ref, dyn_ref, act_ref, cost_ref, out_ref, wide, w_in, w_out, mix
):
    half = weights_ref.shape[0] // 2
    wide[...] = weights_ref[:half].reshape(wide.shape).astype(jnp.float32)
    for j in range(HID // LANES):
        w_in[:, j * LANES : (j + 1) * LANES] = wide[
            pl.ds(j, NS, stride=HID // LANES), :
        ].astype(jnp.bfloat16)
    wide[...] = weights_ref[half:].reshape(wide.shape).astype(jnp.float32)
    for j in range(ACT // LANES):
        w_out[:, j * LANES : (j + 1) * LANES] = wide[
            pl.ds(j, HID, stride=ACT // LANES), :
        ].astype(jnp.bfloat16)
    mix[...] = (
        jnp.dot(w_out[...], act_ref[...], preferred_element_type=jnp.float32) * HID ** (-0.5)
    ).astype(jnp.bfloat16)
    envs = start_ref.shape[0]
    side = NS // 2

    def advance(t, carry):
        states, total = carry
        low = states.astype(jnp.bfloat16)
        hidden = jnp.tanh(
            jnp.dot(low, w_in[...], preferred_element_type=jnp.float32) * NS ** (-0.5)
        ).astype(jnp.bfloat16)
        drifted = jnp.concatenate(
            [
                jnp.dot(
                    low[:, n * side : (n + 1) * side],
                    dyn_ref[n],
                    preferred_element_type=jnp.float32,
                )
                for n in range(2)
            ],
            axis=1,
        )
        states = (
            drifted
            + jnp.dot(hidden, mix[...], preferred_element_type=jnp.float32)
            + pushed_ref[t]
        )
        squares = (states * states).reshape(envs // 8, 8, NS)
        return states, total + jnp.sum(squares, axis=0)

    last, total = lax.fori_loop(
        0, STEPS, advance, (start_ref[...], jnp.zeros((8, NS), jnp.float32))
    )
    weighted = total * cost_ref[...]
    out_ref[...] = jnp.full((8, LANES), jnp.sum(weighted), jnp.float32)


def rollout(weights, start_states, pushed, dyn_pairs, act_map, cost_weights):
    return pl.pallas_call(
        rollout_body,
        out_shape=jax.ShapeDtypeStruct((8, LANES), jnp.float32),
        in_specs=[pl.BlockSpec(memory_space=VMEM)] * 6,
        out_specs=pl.BlockSpec(memory_space=VMEM),
        scratch_shapes=[
            pltpu.VMEM((NS * HID // LANES, LANES), jnp.float32),
            pltpu.VMEM((NS, HID), jnp.bfloat16),
            pltpu.VMEM((HID, ACT), jnp.bfloat16),
            pltpu.VMEM((HID, NS), jnp.bfloat16),
        ],
        compiler_params=pltpu.CompilerParams(vmem_limit_bytes=40 * 1024 * 1024),
        cost_estimate=pl.CostEstimate(
            flops=STEPS * 2 * 64 * NS * 2 * HID * 8, bytes_accessed=8 << 20, transcendentals=1 << 20
        ),
        name="rollout",
    )(weights, start_states, pushed, dyn_pairs, act_map, cost_weights)


def gather_body(count, rows_ref, out_ref, own_sem, send_sem, recv_sem):
    me = lax.axis_index("env")
    right, left = lax.rem(me + 1, count), lax.rem(me + count - 1, count)
    barrier = pltpu.get_barrier_semaphore()
    for peer in (left, right):
        pl.semaphore_signal(
            barrier, inc=1, device_id={"env": peer}, device_id_type=pl.DeviceIdType.MESH
        )
    pl.semaphore_wait(barrier, 2)
    half = rows_ref.shape[0] // 2
    first, second = pl.ds(0, half), pl.ds(half, half)

    def sent(slot, source, owner, part, peer):
        copy = pltpu.make_async_remote_copy(
            src_ref=source.at[part],
            dst_ref=out_ref.at[owner, part],
            send_sem=send_sem.at[slot],
            recv_sem=recv_sem.at[slot],
            device_id={"env": peer},
            device_id_type=pl.DeviceIdType.MESH,
        )
        copy.start()
        return copy

    near_right = sent(0, rows_ref, me, first, right)
    near_left = sent(1, rows_ref, me, second, left)
    rest = [sent(2, rows_ref, me, second, right), sent(3, rows_ref, me, first, left)]
    own = pltpu.make_async_copy(rows_ref, out_ref.at[me], own_sem)
    own.start()
    near_right.wait_recv()
    rest.append(sent(4, out_ref.at[left], left, first, right))
    near_left.wait_recv()
    rest.append(sent(5, out_ref.at[right], right, second, left))
    near_right.wait_send()
    near_left.wait_send()
    for copy in rest:
        copy.wait()
    own.wait()


def gather_env(rows, count):
    return pl.pallas_call(
        functools.partial(gather_body, count),
        out_shape=jax.ShapeDtypeStruct((count, *rows.shape), rows.dtype),
        in_specs=[pl.BlockSpec(memory_space=VMEM)],
        out_specs=pl.BlockSpec(memory_space=VMEM),
        scratch_shapes=[
            pltpu.SemaphoreType.DMA(()),
            pltpu.SemaphoreType.DMA((6,)),
            pltpu.SemaphoreType.DMA((6,)),
        ],
        compiler_params=pltpu.CompilerParams(collective_id=1, has_side_effects=True),
        cost_estimate=pl.CostEstimate(flops=0, bytes_accessed=64 << 20, transcendentals=0),
        name="gather_env",
    )(rows)


PHASES = (("cells_2", "env"), ("cells_1",), ("cells_0",))


def phase_peers(phase, sizes):
    axes = PHASES[phase]
    offsets = [{}]
    for axis in axes:
        offsets = [{**o, axis: d} for o in offsets for d in range(sizes[axis])]
    peers = []
    for offset in offsets[1:]:
        peers.append(
            {a: lax.rem(lax.axis_index(a) + d, sizes[a]) for a, d in offset.items()}
        )
    return peers


def sum_body(sizes, value_ref, out_ref, sums, landed, send_sem, recv_sem):
    everyone = [phase_peers(phase, sizes) for phase in range(len(PHASES))]
    barrier = pltpu.get_barrier_semaphore()
    for peers in everyone:
        for peer in peers:
            pl.semaphore_signal(
                barrier, inc=1, device_id=peer, device_id_type=pl.DeviceIdType.MESH
            )
    pl.semaphore_wait(barrier, sum(len(peers) for peers in everyone))
    sums[0] = value_ref[...]
    for phase, peers in enumerate(everyone):
        copies = []
        for d, peer in enumerate(peers):
            copy = pltpu.make_async_remote_copy(
                src_ref=sums.at[phase],
                dst_ref=landed.at[phase, d],
                send_sem=send_sem.at[phase, d],
                recv_sem=recv_sem.at[phase, d],
                device_id=peer,
                device_id_type=pl.DeviceIdType.MESH,
            )
            copy.start()
            copies.append(copy)
        for copy in copies:
            copy.wait()
        total = sums[phase]
        for d in range(len(peers)):
            total = total + landed[phase, d]
        if phase + 1 < len(PHASES):
            sums[phase + 1] = total
        else:
            out_ref[...] = total


def sum_over_all(value, sizes):
    most = 7
    return pl.pallas_call(
        functools.partial(sum_body, sizes),
        out_shape=jax.ShapeDtypeStruct(value.shape, value.dtype),
        in_specs=[pl.BlockSpec(memory_space=VMEM)],
        out_specs=pl.BlockSpec(memory_space=VMEM),
        scratch_shapes=[
            pltpu.VMEM((len(PHASES), *value.shape), value.dtype),
            pltpu.VMEM((len(PHASES), most, *value.shape), value.dtype),
            pltpu.SemaphoreType.DMA((len(PHASES), most)),
            pltpu.SemaphoreType.DMA((len(PHASES), most)),
        ],
        compiler_params=pltpu.CompilerParams(collective_id=0, has_side_effects=True),
        name="sum_over_all",
    )(value)


def on_device(
    sizes,
    archive,
    fitness_old,
    parents,
    cell_ids,
    replace_mask,
    noise,
    start_states,
    forces,
    dyn_blocks,
    act_map,
    contact_map,
    cost_weights,
):
    cell_dev = archive.shape[0]
    cell_count = lax.axis_size(CELLS)
    total_cells = cell_dev * cell_count
    offspring_count = parents.shape[0]
    position = lax.axis_index(CELLS)
    tiled = (cell_count, SUB, LANES)

    local_ids = position * cell_dev + jnp.arange(cell_dev, dtype=jnp.int32)
    used_local = jnp.any(parents[None, :] == local_ids[:, None], axis=1)
    compact = (
        jnp.dot(used_local[None, :].astype(jnp.bfloat16), archive, preferred_element_type=jnp.float32)
        .astype(jnp.bfloat16)
        .reshape(tiled)
    )
    columns = lax.all_to_all(compact, CELLS, split_axis=0, concat_axis=0, tiled=True)
    parent_cols = pick_tiles(parents // cell_dev, columns)
    parent_rows = lax.all_to_all(parent_cols, CELLS, split_axis=0, concat_axis=0, tiled=True)
    noise_tiles = noise[0].reshape(tiled)
    children = (parent_rows.astype(jnp.float32) + noise_tiles.astype(jnp.float32)).astype(
        jnp.bfloat16
    )

    cell_range = jnp.arange(total_cells, dtype=jnp.int32)
    matches = cell_ids[None, :] == cell_range[:, None]
    eligible = matches & (replace_mask[None, :] == 1)
    indices = jnp.arange(offspring_count, dtype=jnp.int32)
    winner = jnp.max(jnp.where(eligible, indices[None, :], -1), axis=1)
    winning = indices[None, :] == winner[:, None]
    chosen = winner >= 0

    child_cols = lax.all_to_all(children, CELLS, split_axis=0, concat_axis=0, tiled=True)
    weights = gather_env(children, sizes["env"])
    placed = jnp.dot(
        winning.astype(jnp.bfloat16),
        child_cols.reshape(cell_count, SUB * LANES),
        preferred_element_type=jnp.float32,
    ).astype(jnp.bfloat16)
    weights, placed = lax.optimization_barrier((weights, placed))
    replaced = lax.all_to_all(
        placed.reshape(cell_count, cell_dev, SUB * LANES),
        CELLS,
        split_axis=0,
        concat_axis=0,
        tiled=True,
    )
    replaced = jnp.moveaxis(replaced, 1, 0).reshape(archive.shape)
    own_chosen = lax.dynamic_slice_in_dim(chosen, position * cell_dev, cell_dev, 0)
    new_archive = jnp.where(own_chosen[:, None], replaced, archive)

    envs = start_states.shape[0]
    pushed = jnp.dot(
        forces.reshape(STEPS * envs, -1), contact_map, preferred_element_type=jnp.float32
    ).reshape(STEPS, envs, NS)
    dyn_pairs = (
        dyn_blocks.reshape(2, 2, BLK, 1, BLK)
        * jnp.eye(2, dtype=jnp.bfloat16)[None, :, None, :, None]
    ).reshape(2, 2 * BLK, 2 * BLK)
    cost = rollout(
        weights, start_states, pushed, dyn_pairs, act_map, cost_weights.reshape(1, NS)
    )
    slots = jnp.where(indices[None, :] == position, cost, 0.0)
    all_costs = sum_over_all(slots, sizes)[0]

    envs_total = envs * lax.axis_size("env")
    fitness = -all_costs / (STEPS * envs_total * NS)
    own_winning = lax.dynamic_slice_in_dim(winning, position * cell_dev, cell_dev, 0)
    own_matches = lax.dynamic_slice_in_dim(matches, position * cell_dev, cell_dev, 0)
    winner_fitness = jnp.sum(jnp.where(own_winning, fitness[None, :], 0.0), axis=1)
    new_fitness = jnp.where(own_chosen, winner_fitness, fitness_old)
    lifted = jnp.maximum(fitness[None, :] - fitness_old[:, None], 0.0)
    cell_gain = jnp.sum(jnp.where(own_matches, lifted, 0.0), axis=1)
    return (new_archive, new_fitness, cell_gain)


def solution(mesh):
    split = Mesh(
        mesh.devices.reshape(8, 8, 2, mesh.shape["env"]), ("cells_0", "cells_1", "cells_2", "env")
    )
    return jax.shard_map(
        functools.partial(on_device, dict(split.shape)),
        mesh=split,
        in_specs=(
            P(CELLS, "env"),
            P(CELLS),
            P(),
            P(),
            P(),
            P(CELLS, "env"),
            P("env", None),
            P(None, "env", None),
            P(),
            P(),
            P(),
            P(),
        ),
        out_specs=(P(CELLS, "env"), P(CELLS), P(CELLS)),
        check_vma=False,
    )
```

```python
import functools

import jax
import jax.numpy as jnp
from jax import lax
from jax.experimental import pallas as pl
from jax.experimental.pallas import tpu as pltpu
from jax.sharding import Mesh
from jax.sharding import PartitionSpec as P

NS = 512
HID = 1024
ACT = 512
BLK = 128
STEPS = 16
CELLS = ("cells_0", "cells_1", "cells_2")
LANES = 128
SUB = 16
VMEM = pltpu.MemorySpace.VMEM
SMEM = pltpu.MemorySpace.SMEM


MESH = pl.DeviceIdType.MESH


def cell_peer(step, sizes):
    rows, columns, cores = (sizes[a] for a in CELLS)
    mixed = lax.rem(step * 37, rows * columns * cores)
    row = lax.rem(lax.axis_index("cells_0") + lax.div(mixed, columns * cores), rows)
    column = lax.rem(
        lax.axis_index("cells_1") + lax.rem(lax.div(mixed, cores), columns), columns
    )
    core = lax.rem(lax.axis_index("cells_2") + lax.rem(mixed, cores), cores)
    peer = {"cells_0": row, "cells_1": column, "cells_2": core}
    return peer, (row * columns + column) * cores + core


def own_cell(sizes):
    return (
        lax.axis_index("cells_0") * sizes["cells_1"] + lax.axis_index("cells_1")
    ) * sizes["cells_2"] + lax.axis_index("cells_2")


def greet_cells(barrier, sizes, count):
    def one(step, carry):
        peer, _ = cell_peer(step, sizes)
        pl.semaphore_signal(barrier, inc=1, device_id=peer, device_id_type=MESH)
        return carry

    lax.fori_loop(1, count, one, 0)


def start_exchange(sizes, source, target, own_sem, send_sem, recv_sem):
    count = source.shape[0]
    me = own_cell(sizes)

    def one(step, carry):
        peer, index = cell_peer(step, sizes)
        pltpu.make_async_remote_copy(
            src_ref=source.at[index],
            dst_ref=target.at[me],
            send_sem=send_sem,
            recv_sem=recv_sem,
            device_id=peer,
            device_id_type=MESH,
        ).start()
        return carry

    lax.fori_loop(1, count, one, 0)
    own = pltpu.make_async_copy(source.at[me], target.at[me], own_sem)
    own.start()

    def finish():
        others = pl.ds(0, count - 1)
        pltpu.make_async_copy(source.at[others], target.at[others], recv_sem).wait()
        pltpu.make_async_copy(source.at[others], target.at[others], send_sem).wait()
        own.wait()

    return finish


def route_body(sizes, index_ref, rows_ref, out_ref, columns, picked, own_sem, send_sem, recv_sem):
    count = rows_ref.shape[0]
    barrier = pltpu.get_barrier_semaphore()
    greet_cells(barrier, sizes, count)
    pl.semaphore_wait(barrier, count - 1)
    start_exchange(sizes, rows_ref, columns, own_sem.at[0], send_sem.at[0], recv_sem.at[0])()

    def one(k, carry):
        picked[k] = columns[index_ref[k]]
        return carry

    lax.fori_loop(0, count, one, 0)
    start_exchange(sizes, picked, out_ref, own_sem.at[1], send_sem.at[1], recv_sem.at[1])()


def route_parents(index, rows, sizes):
    return pl.pallas_call(
        functools.partial(route_body, sizes),
        out_shape=jax.ShapeDtypeStruct(rows.shape, rows.dtype),
        in_specs=[pl.BlockSpec(memory_space=SMEM), pl.BlockSpec(memory_space=VMEM)],
        out_specs=pl.BlockSpec(memory_space=VMEM),
        scratch_shapes=[
            pltpu.VMEM(rows.shape, rows.dtype),
            pltpu.VMEM(rows.shape, rows.dtype),
            pltpu.SemaphoreType.DMA((2,)),
            pltpu.SemaphoreType.DMA((2,)),
            pltpu.SemaphoreType.DMA((2,)),
        ],
        compiler_params=pltpu.CompilerParams(collective_id=1, has_side_effects=True),
        name="route_parents",
    )(index, rows)


def rollout_body(
    weights_ref, start_ref, pushed_ref, dyn_ref, act_ref, cost_ref, out_ref, wide, w_in, w_out, mix
):
    half = weights_ref.shape[0] // 2
    wide[...] = weights_ref[:half].reshape(wide.shape).astype(jnp.float32)
    for j in range(HID // LANES):
        w_in[:, j * LANES : (j + 1) * LANES] = wide[
            pl.ds(j, NS, stride=HID // LANES), :
        ].astype(jnp.bfloat16)
    wide[...] = weights_ref[half:].reshape(wide.shape).astype(jnp.float32)
    for j in range(ACT // LANES):
        w_out[:, j * LANES : (j + 1) * LANES] = wide[
            pl.ds(j, HID, stride=ACT // LANES), :
        ].astype(jnp.bfloat16)
    mix[...] = (
        jnp.dot(w_out[...], act_ref[...], preferred_element_type=jnp.float32) * HID ** (-0.5)
    ).astype(jnp.bfloat16)
    envs = start_ref.shape[0]
    side = NS // 2

    def advance(t, carry):
        states, total = carry
        low = states.astype(jnp.bfloat16)
        hidden = jnp.tanh(
            jnp.dot(low, w_in[...], preferred_element_type=jnp.float32) * NS ** (-0.5)
        ).astype(jnp.bfloat16)
        drifted = jnp.concatenate(
            [
                jnp.dot(
                    low[:, n * side : (n + 1) * side],
                    dyn_ref[n],
                    preferred_element_type=jnp.float32,
                )
                for n in range(2)
            ],
            axis=1,
        )
        states = (
            drifted
            + jnp.dot(hidden, mix[...], preferred_element_type=jnp.float32)
            + pushed_ref[t]
        )
        squares = (states * states).reshape(envs // 8, 8, NS)
        return states, total + jnp.sum(squares, axis=0)

    last, total = lax.fori_loop(
        0, STEPS, advance, (start_ref[...], jnp.zeros((8, NS), jnp.float32))
    )
    weighted = total * cost_ref[...]
    out_ref[...] = jnp.full((8, LANES), jnp.sum(weighted), jnp.float32)


def rollout(weights, start_states, pushed, dyn_pairs, act_map, cost_weights):
    return pl.pallas_call(
        rollout_body,
        out_shape=jax.ShapeDtypeStruct((8, LANES), jnp.float32),
        in_specs=[pl.BlockSpec(memory_space=VMEM)] * 6,
        out_specs=pl.BlockSpec(memory_space=VMEM),
        scratch_shapes=[
            pltpu.VMEM((NS * HID // LANES, LANES), jnp.float32),
            pltpu.VMEM((NS, HID), jnp.bfloat16),
            pltpu.VMEM((HID, ACT), jnp.bfloat16),
            pltpu.VMEM((HID, NS), jnp.bfloat16),
        ],
        compiler_params=pltpu.CompilerParams(vmem_limit_bytes=40 * 1024 * 1024),
        cost_estimate=pl.CostEstimate(
            flops=STEPS * 2 * 64 * NS * 2 * HID * 8, bytes_accessed=8 << 20, transcendentals=1 << 20
        ),
        name="rollout",
    )(weights, start_states, pushed, dyn_pairs, act_map, cost_weights)


def spread_body(sizes, rows_ref, out_ref, columns_ref, own_sem, send_sem, recv_sem):
    count = sizes["env"]
    me = lax.axis_index("env")
    right, left = lax.rem(me + 1, count), lax.rem(me + count - 1, count)
    barrier = pltpu.get_barrier_semaphore()
    for peer in (left, right):
        pl.semaphore_signal(barrier, inc=1, device_id={"env": peer}, device_id_type=MESH)
    greet_cells(barrier, sizes, rows_ref.shape[0])
    pl.semaphore_wait(barrier, rows_ref.shape[0] + 1)
    half = rows_ref.shape[0] // 2
    first, second = pl.ds(0, half), pl.ds(half, half)

    def sent(slot, source, owner, part, peer):
        copy = pltpu.make_async_remote_copy(
            src_ref=source.at[part],
            dst_ref=out_ref.at[owner, part],
            send_sem=send_sem.at[slot],
            recv_sem=recv_sem.at[slot],
            device_id={"env": peer},
            device_id_type=MESH,
        )
        copy.start()
        return copy

    near_right = sent(0, rows_ref, me, first, right)
    near_left = sent(1, rows_ref, me, second, left)
    rest = [sent(2, rows_ref, me, second, right), sent(3, rows_ref, me, first, left)]
    finish = start_exchange(
        sizes, rows_ref, columns_ref, own_sem.at[0], send_sem.at[6], recv_sem.at[6]
    )
    own = pltpu.make_async_copy(rows_ref, out_ref.at[me], own_sem.at[1])
    own.start()
    near_right.wait_recv()
    rest.append(sent(4, out_ref.at[left], left, first, right))
    near_left.wait_recv()
    rest.append(sent(5, out_ref.at[right], right, second, left))
    near_right.wait_send()
    near_left.wait_send()
    for copy in rest:
        copy.wait()
    own.wait()
    finish()


def spread_children(rows, sizes):
    return pl.pallas_call(
        functools.partial(spread_body, sizes),
        out_shape=(
            jax.ShapeDtypeStruct((sizes["env"], *rows.shape), rows.dtype),
            jax.ShapeDtypeStruct(rows.shape, rows.dtype),
        ),
        in_specs=[pl.BlockSpec(memory_space=VMEM)],
        out_specs=(pl.BlockSpec(memory_space=VMEM), pl.BlockSpec(memory_space=VMEM)),
        scratch_shapes=[
            pltpu.SemaphoreType.DMA((2,)),
            pltpu.SemaphoreType.DMA((7,)),
            pltpu.SemaphoreType.DMA((7,)),
        ],
        compiler_params=pltpu.CompilerParams(collective_id=2, has_side_effects=True),
        name="spread_children",
    )(rows)


PHASES = (("cells_2", "env"), ("cells_1",), ("cells_0",))


def phase_peers(phase, sizes):
    axes = PHASES[phase]
    offsets = [{}]
    for axis in axes:
        offsets = [{**o, axis: d} for o in offsets for d in range(sizes[axis])]
    peers = []
    for offset in offsets[1:]:
        peers.append(
            {a: lax.rem(lax.axis_index(a) + d, sizes[a]) for a, d in offset.items()}
        )
    return peers


def sum_body(sizes, value_ref, out_ref, sums, landed, send_sem, recv_sem):
    everyone = [phase_peers(phase, sizes) for phase in range(len(PHASES))]
    barrier = pltpu.get_barrier_semaphore()
    for peers in everyone:
        for peer in peers:
            pl.semaphore_signal(
                barrier, inc=1, device_id=peer, device_id_type=pl.DeviceIdType.MESH
            )
    pl.semaphore_wait(barrier, sum(len(peers) for peers in everyone))
    sums[0] = value_ref[...]
    for phase, peers in enumerate(everyone):
        copies = []
        for d, peer in enumerate(peers):
            copy = pltpu.make_async_remote_copy(
                src_ref=sums.at[phase],
                dst_ref=landed.at[phase, d],
                send_sem=send_sem.at[phase, d],
                recv_sem=recv_sem.at[phase, d],
                device_id=peer,
                device_id_type=pl.DeviceIdType.MESH,
            )
            copy.start()
            copies.append(copy)
        for copy in copies:
            copy.wait()
        total = sums[phase]
        for d in range(len(peers)):
            total = total + landed[phase, d]
        if phase + 1 < len(PHASES):
            sums[phase + 1] = total
        else:
            out_ref[...] = total


def sum_over_all(value, sizes):
    most = 7
    return pl.pallas_call(
        functools.partial(sum_body, sizes),
        out_shape=jax.ShapeDtypeStruct(value.shape, value.dtype),
        in_specs=[pl.BlockSpec(memory_space=VMEM)],
        out_specs=pl.BlockSpec(memory_space=VMEM),
        scratch_shapes=[
            pltpu.VMEM((len(PHASES), *value.shape), value.dtype),
            pltpu.VMEM((len(PHASES), most, *value.shape), value.dtype),
            pltpu.SemaphoreType.DMA((len(PHASES), most)),
            pltpu.SemaphoreType.DMA((len(PHASES), most)),
        ],
        compiler_params=pltpu.CompilerParams(collective_id=0, has_side_effects=True),
        name="sum_over_all",
    )(value)


def on_device(
    sizes,
    archive,
    fitness_old,
    parents,
    cell_ids,
    replace_mask,
    noise,
    start_states,
    forces,
    dyn_blocks,
    act_map,
    contact_map,
    cost_weights,
):
    cell_dev = archive.shape[0]
    cell_count = lax.axis_size(CELLS)
    total_cells = cell_dev * cell_count
    offspring_count = parents.shape[0]
    position = lax.axis_index(CELLS)
    tiled = (cell_count, SUB, LANES)

    local_ids = position * cell_dev + jnp.arange(cell_dev, dtype=jnp.int32)
    used_local = jnp.any(parents[None, :] == local_ids[:, None], axis=1)
    compact = (
        jnp.dot(used_local[None, :].astype(jnp.bfloat16), archive, preferred_element_type=jnp.float32)
        .astype(jnp.bfloat16)
        .reshape(tiled)
    )
    parent_rows = route_parents(parents // cell_dev, compact, sizes)
    noise_tiles = noise[0].reshape(tiled)
    children = (parent_rows.astype(jnp.float32) + noise_tiles.astype(jnp.float32)).astype(
        jnp.bfloat16
    )

    cell_range = jnp.arange(total_cells, dtype=jnp.int32)
    matches = cell_ids[None, :] == cell_range[:, None]
    eligible = matches & (replace_mask[None, :] == 1)
    indices = jnp.arange(offspring_count, dtype=jnp.int32)
    winner = jnp.max(jnp.where(eligible, indices[None, :], -1), axis=1)
    winning = indices[None, :] == winner[:, None]
    chosen = winner >= 0

    weights, child_cols = spread_children(children, sizes)
    placed = jnp.dot(
        winning.astype(jnp.bfloat16),
        child_cols.reshape(cell_count, SUB * LANES),
        preferred_element_type=jnp.float32,
    ).astype(jnp.bfloat16)
    weights, placed = lax.optimization_barrier((weights, placed))
    replaced = lax.all_to_all(
        placed.reshape(cell_count, cell_dev, SUB * LANES),
        CELLS,
        split_axis=0,
        concat_axis=0,
        tiled=True,
    )
    replaced = jnp.moveaxis(replaced, 1, 0).reshape(archive.shape)
    own_chosen = lax.dynamic_slice_in_dim(chosen, position * cell_dev, cell_dev, 0)
    new_archive = jnp.where(own_chosen[:, None], replaced, archive)

    envs = start_states.shape[0]
    pushed = jnp.dot(
        forces.reshape(STEPS * envs, -1), contact_map, preferred_element_type=jnp.float32
    ).reshape(STEPS, envs, NS)
    dyn_pairs = (
        dyn_blocks.reshape(2, 2, BLK, 1, BLK)
        * jnp.eye(2, dtype=jnp.bfloat16)[None, :, None, :, None]
    ).reshape(2, 2 * BLK, 2 * BLK)
    cost = rollout(
        weights, start_states, pushed, dyn_pairs, act_map, cost_weights.reshape(1, NS)
    )
    slots = jnp.where(indices[None, :] == position, cost, 0.0)
    all_costs = sum_over_all(slots, sizes)[0]

    envs_total = envs * lax.axis_size("env")
    fitness = -all_costs / (STEPS * envs_total * NS)
    own_winning = lax.dynamic_slice_in_dim(winning, position * cell_dev, cell_dev, 0)
    own_matches = lax.dynamic_slice_in_dim(matches, position * cell_dev, cell_dev, 0)
    winner_fitness = jnp.sum(jnp.where(own_winning, fitness[None, :], 0.0), axis=1)
    new_fitness = jnp.where(own_chosen, winner_fitness, fitness_old)
    lifted = jnp.maximum(fitness[None, :] - fitness_old[:, None], 0.0)
    cell_gain = jnp.sum(jnp.where(own_matches, lifted, 0.0), axis=1)
    return (new_archive, new_fitness, cell_gain)


def solution(mesh):
    split = Mesh(
        mesh.devices.reshape(8, 8, 2, mesh.shape["env"]), ("cells_0", "cells_1", "cells_2", "env")
    )
    return jax.shard_map(
        functools.partial(on_device, dict(split.shape)),
        mesh=split,
        in_specs=(
            P(CELLS, "env"),
            P(CELLS),
            P(),
            P(),
            P(),
            P(CELLS, "env"),
            P("env", None),
            P(None, "env", None),
            P(),
            P(),
            P(),
            P(),
        ),
        out_specs=(P(CELLS, "env"), P(CELLS), P(CELLS)),
        check_vma=False,
    )
```

```python
import functools

import jax
import jax.numpy as jnp
from jax import lax
from jax.experimental import pallas as pl
from jax.experimental.pallas import tpu as pltpu
from jax.sharding import Mesh
from jax.sharding import PartitionSpec as P

NS = 512
HID = 1024
ACT = 512
BLK = 128
STEPS = 16
CELLS = ("cells_0", "cells_1", "cells_2")
LANES = 128
SUB = 16
VMEM = pltpu.MemorySpace.VMEM
SMEM = pltpu.MemorySpace.SMEM


MESH = pl.DeviceIdType.MESH


def cell_peer(step, sizes):
    rows, columns, cores = (sizes[a] for a in CELLS)
    mixed = lax.rem(step * 37, rows * columns * cores)
    row = lax.rem(lax.axis_index("cells_0") + lax.div(mixed, columns * cores), rows)
    column = lax.rem(
        lax.axis_index("cells_1") + lax.rem(lax.div(mixed, cores), columns), columns
    )
    core = lax.rem(lax.axis_index("cells_2") + lax.rem(mixed, cores), cores)
    peer = {"cells_0": row, "cells_1": column, "cells_2": core}
    return peer, (row * columns + column) * cores + core


def own_cell(sizes):
    return (
        lax.axis_index("cells_0") * sizes["cells_1"] + lax.axis_index("cells_1")
    ) * sizes["cells_2"] + lax.axis_index("cells_2")


def greet_cells(barrier, sizes, count):
    def one(step, carry):
        peer, _ = cell_peer(step, sizes)
        pl.semaphore_signal(barrier, inc=1, device_id=peer, device_id_type=MESH)
        return carry

    lax.fori_loop(1, count, one, 0)


def start_exchange(sizes, source, target, own_sem, send_sem, recv_sem):
    count = source.shape[0]
    me = own_cell(sizes)

    def one(step, carry):
        peer, index = cell_peer(step, sizes)
        pltpu.make_async_remote_copy(
            src_ref=source.at[index],
            dst_ref=target.at[me],
            send_sem=send_sem,
            recv_sem=recv_sem,
            device_id=peer,
            device_id_type=MESH,
        ).start()
        return carry

    lax.fori_loop(1, count, one, 0)
    own = pltpu.make_async_copy(source.at[me], target.at[me], own_sem)
    own.start()

    def finish():
        others = pl.ds(0, count - 1)
        pltpu.make_async_copy(source.at[others], target.at[others], recv_sem).wait()
        pltpu.make_async_copy(source.at[others], target.at[others], send_sem).wait()
        own.wait()

    return finish


def column_body(
    sizes, index_ref, parent_ref, noise_ref, out_ref, pairs, columns, own_sem, send_sem, recv_sem
):
    count = pairs.shape[0]
    barrier = pltpu.get_barrier_semaphore()
    greet_cells(barrier, sizes, count)
    pairs[:, 0] = parent_ref[...].astype(pairs.dtype)
    pairs[:, 1] = noise_ref[...].astype(pairs.dtype)
    pl.semaphore_wait(barrier, count - 1)
    start_exchange(sizes, pairs, columns, own_sem, send_sem, recv_sem)()

    def one(k, carry):
        parent = columns[index_ref[k], 0].astype(jnp.float32)
        out_ref[k] = (parent + columns[k, 1].astype(jnp.float32)).astype(out_ref.dtype)
        return carry

    lax.fori_loop(0, count, one, 0)


def child_columns(index, parent, noise, sizes):
    count, *tile = parent.shape
    both = pltpu.VMEM((count, 2, *tile), jnp.bfloat16)
    return pl.pallas_call(
        functools.partial(column_body, sizes),
        out_shape=jax.ShapeDtypeStruct((count, *tile), jnp.bfloat16),
        in_specs=[pl.BlockSpec(memory_space=SMEM)] + [pl.BlockSpec(memory_space=VMEM)] * 2,
        out_specs=pl.BlockSpec(memory_space=VMEM),
        scratch_shapes=[
            both,
            both,
            pltpu.SemaphoreType.DMA(()),
            pltpu.SemaphoreType.DMA(()),
            pltpu.SemaphoreType.DMA(()),
        ],
        compiler_params=pltpu.CompilerParams(collective_id=1, has_side_effects=True),
        name="child_columns",
    )(index, parent, noise)


def rollout_body(
    weights_ref, start_ref, pushed_ref, dyn_ref, act_ref, cost_ref, out_ref, wide, w_in, w_out, mix
):
    half = weights_ref.shape[0] // 2
    wide[...] = weights_ref[:half].reshape(wide.shape).astype(jnp.float32)
    for j in range(HID // LANES):
        w_in[:, j * LANES : (j + 1) * LANES] = wide[
            pl.ds(j, NS, stride=HID // LANES), :
        ].astype(jnp.bfloat16)
    wide[...] = weights_ref[half:].reshape(wide.shape).astype(jnp.float32)
    for j in range(ACT // LANES):
        w_out[:, j * LANES : (j + 1) * LANES] = wide[
            pl.ds(j, HID, stride=ACT // LANES), :
        ].astype(jnp.bfloat16)
    mix[...] = (
        jnp.dot(w_out[...], act_ref[...], preferred_element_type=jnp.float32) * HID ** (-0.5)
    ).astype(jnp.bfloat16)
    envs = start_ref.shape[0]
    side = NS // 2

    def advance(t, carry):
        states, total = carry
        low = states.astype(jnp.bfloat16)
        hidden = jnp.tanh(
            jnp.dot(low, w_in[...], preferred_element_type=jnp.float32) * NS ** (-0.5)
        ).astype(jnp.bfloat16)
        drifted = jnp.concatenate(
            [
                jnp.dot(
                    low[:, n * side : (n + 1) * side],
                    dyn_ref[n],
                    preferred_element_type=jnp.float32,
                )
                for n in range(2)
            ],
            axis=1,
        )
        states = (
            drifted
            + jnp.dot(hidden, mix[...], preferred_element_type=jnp.float32)
            + pushed_ref[t]
        )
        squares = (states * states).reshape(envs // 8, 8, NS)
        return states, total + jnp.sum(squares, axis=0)

    last, total = lax.fori_loop(
        0, STEPS, advance, (start_ref[...], jnp.zeros((8, NS), jnp.float32))
    )
    weighted = total * cost_ref[...]
    out_ref[...] = jnp.full((8, LANES), jnp.sum(weighted), jnp.float32)


def rollout(weights, start_states, pushed, dyn_pairs, act_map, cost_weights):
    return pl.pallas_call(
        rollout_body,
        out_shape=jax.ShapeDtypeStruct((8, LANES), jnp.float32),
        in_specs=[pl.BlockSpec(memory_space=VMEM)] * 6,
        out_specs=pl.BlockSpec(memory_space=VMEM),
        scratch_shapes=[
            pltpu.VMEM((NS * HID // LANES, LANES), jnp.float32),
            pltpu.VMEM((NS, HID), jnp.bfloat16),
            pltpu.VMEM((HID, ACT), jnp.bfloat16),
            pltpu.VMEM((HID, NS), jnp.bfloat16),
        ],
        compiler_params=pltpu.CompilerParams(vmem_limit_bytes=40 * 1024 * 1024),
        cost_estimate=pl.CostEstimate(
            flops=STEPS * 2 * 64 * NS * 2 * HID * 8, bytes_accessed=8 << 20, transcendentals=1 << 20
        ),
        name="rollout",
    )(weights, start_states, pushed, dyn_pairs, act_map, cost_weights)


def spread_body(
    sizes, columns_ref, placed_ref, out_ref, replaced_ref, own_sem, send_sem, recv_sem
):
    count = sizes["env"]
    me = lax.axis_index("env")
    right, left = lax.rem(me + 1, count), lax.rem(me + count - 1, count)
    cells = columns_ref.shape[0]
    barrier = pltpu.get_barrier_semaphore()
    for peer in (left, right):
        pl.semaphore_signal(barrier, inc=1, device_id={"env": peer}, device_id_type=MESH)
    greet_cells(barrier, sizes, cells)
    pl.semaphore_wait(barrier, cells + 1)
    half = cells // 2
    first, second = pl.ds(0, half), pl.ds(half, half)

    def sent(slot, owner, part, peer):
        copy = pltpu.make_async_remote_copy(
            src_ref=out_ref.at[owner, part],
            dst_ref=out_ref.at[owner, part],
            send_sem=send_sem.at[slot],
            recv_sem=recv_sem.at[slot],
            device_id={"env": peer},
            device_id_type=MESH,
        )
        copy.start()
        return copy

    rows_here = start_exchange(
        sizes, columns_ref, out_ref.at[me], own_sem.at[0], send_sem.at[6], recv_sem.at[6]
    )
    replaced_here = start_exchange(
        sizes, placed_ref, replaced_ref, own_sem.at[1], send_sem.at[7], recv_sem.at[7]
    )
    rows_here()
    near_right = sent(0, me, first, right)
    near_left = sent(1, me, second, left)
    rest = [sent(2, me, second, right), sent(3, me, first, left)]
    near_right.wait_recv()
    rest.append(sent(4, left, first, right))
    near_left.wait_recv()
    rest.append(sent(5, right, second, left))
    near_right.wait_send()
    near_left.wait_send()
    for copy in rest:
        copy.wait()
    replaced_here()


def spread_children(columns, placed, sizes):
    return pl.pallas_call(
        functools.partial(spread_body, sizes),
        out_shape=(
            jax.ShapeDtypeStruct((sizes["env"], *columns.shape), columns.dtype),
            jax.ShapeDtypeStruct(placed.shape, placed.dtype),
        ),
        in_specs=[pl.BlockSpec(memory_space=VMEM)] * 2,
        out_specs=(pl.BlockSpec(memory_space=VMEM), pl.BlockSpec(memory_space=VMEM)),
        scratch_shapes=[
            pltpu.SemaphoreType.DMA((2,)),
            pltpu.SemaphoreType.DMA((8,)),
            pltpu.SemaphoreType.DMA((8,)),
        ],
        compiler_params=pltpu.CompilerParams(collective_id=2, has_side_effects=True),
        name="spread_children",
    )(columns, placed)


PHASES = (("cells_2", "env"), ("cells_1",), ("cells_0",))


def phase_peers(phase, sizes):
    axes = PHASES[phase]
    offsets = [{}]
    for axis in axes:
        offsets = [{**o, axis: d} for o in offsets for d in range(sizes[axis])]
    peers = []
    for offset in offsets[1:]:
        peers.append(
            {a: lax.rem(lax.axis_index(a) + d, sizes[a]) for a, d in offset.items()}
        )
    return peers


def sum_body(sizes, value_ref, out_ref, sums, landed, send_sem, recv_sem):
    everyone = [phase_peers(phase, sizes) for phase in range(len(PHASES))]
    barrier = pltpu.get_barrier_semaphore()
    for peers in everyone:
        for peer in peers:
            pl.semaphore_signal(
                barrier, inc=1, device_id=peer, device_id_type=pl.DeviceIdType.MESH
            )
    pl.semaphore_wait(barrier, sum(len(peers) for peers in everyone))
    sums[0] = value_ref[...]
    for phase, peers in enumerate(everyone):
        copies = []
        for d, peer in enumerate(peers):
            copy = pltpu.make_async_remote_copy(
                src_ref=sums.at[phase],
                dst_ref=landed.at[phase, d],
                send_sem=send_sem.at[phase, d],
                recv_sem=recv_sem.at[phase, d],
                device_id=peer,
                device_id_type=pl.DeviceIdType.MESH,
            )
            copy.start()
            copies.append(copy)
        for copy in copies:
            copy.wait()
        total = sums[phase]
        for d in range(len(peers)):
            total = total + landed[phase, d]
        if phase + 1 < len(PHASES):
            sums[phase + 1] = total
        else:
            out_ref[...] = total


def sum_over_all(value, sizes):
    most = 7
    return pl.pallas_call(
        functools.partial(sum_body, sizes),
        out_shape=jax.ShapeDtypeStruct(value.shape, value.dtype),
        in_specs=[pl.BlockSpec(memory_space=VMEM)],
        out_specs=pl.BlockSpec(memory_space=VMEM),
        scratch_shapes=[
            pltpu.VMEM((len(PHASES), *value.shape), value.dtype),
            pltpu.VMEM((len(PHASES), most, *value.shape), value.dtype),
            pltpu.SemaphoreType.DMA((len(PHASES), most)),
            pltpu.SemaphoreType.DMA((len(PHASES), most)),
        ],
        compiler_params=pltpu.CompilerParams(collective_id=0, has_side_effects=True),
        name="sum_over_all",
    )(value)


def on_device(
    sizes,
    archive,
    fitness_old,
    parents,
    cell_ids,
    replace_mask,
    noise,
    start_states,
    forces,
    dyn_blocks,
    act_map,
    contact_map,
    cost_weights,
):
    cell_dev = archive.shape[0]
    cell_count = lax.axis_size(CELLS)
    total_cells = cell_dev * cell_count
    offspring_count = parents.shape[0]
    position = lax.axis_index(CELLS)
    tiled = (cell_count, SUB, LANES)

    local_ids = position * cell_dev + jnp.arange(cell_dev, dtype=jnp.int32)
    used_local = jnp.any(parents[None, :] == local_ids[:, None], axis=1)
    compact = jnp.dot(
        used_local[None, :].astype(jnp.bfloat16), archive, preferred_element_type=jnp.float32
    )
    compact = lax.optimization_barrier(compact)
    spread = noise.astype(jnp.float32)
    child_cols = child_columns(
        parents // cell_dev, compact.reshape(tiled), spread.reshape(tiled), sizes
    )

    cell_range = jnp.arange(total_cells, dtype=jnp.int32)
    matches = cell_ids[None, :] == cell_range[:, None]
    eligible = matches & (replace_mask[None, :] == 1)
    indices = jnp.arange(offspring_count, dtype=jnp.int32)
    winner = jnp.max(jnp.where(eligible, indices[None, :], -1), axis=1)
    winning = indices[None, :] == winner[:, None]
    chosen = winner >= 0

    placed = jnp.dot(
        winning.astype(jnp.bfloat16),
        child_cols.reshape(cell_count, SUB * LANES),
        preferred_element_type=jnp.float32,
    ).astype(jnp.bfloat16)
    weights, replaced = spread_children(
        child_cols, placed.reshape(cell_count, cell_dev, SUB * LANES), sizes
    )
    replaced = jnp.moveaxis(replaced, 1, 0).reshape(archive.shape)
    own_chosen = lax.dynamic_slice_in_dim(chosen, position * cell_dev, cell_dev, 0)
    new_archive = jnp.where(own_chosen[:, None], replaced, archive)

    envs = start_states.shape[0]
    pushed = jnp.dot(
        forces.reshape(STEPS * envs, -1), contact_map, preferred_element_type=jnp.float32
    ).reshape(STEPS, envs, NS)
    dyn_pairs = (
        dyn_blocks.reshape(2, 2, BLK, 1, BLK)
        * jnp.eye(2, dtype=jnp.bfloat16)[None, :, None, :, None]
    ).reshape(2, 2 * BLK, 2 * BLK)
    cost = rollout(
        weights, start_states, pushed, dyn_pairs, act_map, cost_weights.reshape(1, NS)
    )
    slots = jnp.where(indices[None, :] == position, cost, 0.0)
    all_costs = sum_over_all(slots, sizes)[0]

    envs_total = envs * lax.axis_size("env")
    fitness = -all_costs / (STEPS * envs_total * NS)
    own_winning = lax.dynamic_slice_in_dim(winning, position * cell_dev, cell_dev, 0)
    own_matches = lax.dynamic_slice_in_dim(matches, position * cell_dev, cell_dev, 0)
    winner_fitness = jnp.sum(jnp.where(own_winning, fitness[None, :], 0.0), axis=1)
    new_fitness = jnp.where(own_chosen, winner_fitness, fitness_old)
    lifted = jnp.maximum(fitness[None, :] - fitness_old[:, None], 0.0)
    cell_gain = jnp.sum(jnp.where(own_matches, lifted, 0.0), axis=1)
    return (new_archive, new_fitness, cell_gain)


def solution(mesh):
    split = Mesh(
        mesh.devices.reshape(8, 8, 2, mesh.shape["env"]), ("cells_0", "cells_1", "cells_2", "env")
    )
    return jax.shard_map(
        functools.partial(on_device, dict(split.shape)),
        mesh=split,
        in_specs=(
            P(CELLS, "env"),
            P(CELLS),
            P(),
            P(),
            P(),
            P(CELLS, "env"),
            P("env", None),
            P(None, "env", None),
            P(),
            P(),
            P(),
            P(),
        ),
        out_specs=(P(CELLS, "env"), P(CELLS), P(CELLS)),
        check_vma=False,
    )
```

```python
import functools

import jax
import jax.numpy as jnp
from jax import lax
from jax.experimental import pallas as pl
from jax.experimental.pallas import tpu as pltpu
from jax.sharding import Mesh
from jax.sharding import PartitionSpec as P

NS = 512
HID = 1024
ACT = 512
BLK = 128
STEPS = 16
CELLS = ("cells_0", "cells_1", "cells_2")
LANES = 128
SUB = 16
VMEM = pltpu.MemorySpace.VMEM
SMEM = pltpu.MemorySpace.SMEM


MESH = pl.DeviceIdType.MESH


def cell_peer(step, sizes):
    rows, columns, cores = (sizes[a] for a in CELLS)
    mixed = lax.rem(step * 37, rows * columns * cores)
    row = lax.rem(lax.axis_index("cells_0") + lax.div(mixed, columns * cores), rows)
    column = lax.rem(
        lax.axis_index("cells_1") + lax.rem(lax.div(mixed, cores), columns), columns
    )
    core = lax.rem(lax.axis_index("cells_2") + lax.rem(mixed, cores), cores)
    peer = {"cells_0": row, "cells_1": column, "cells_2": core}
    return peer, (row * columns + column) * cores + core


def own_cell(sizes):
    return (
        lax.axis_index("cells_0") * sizes["cells_1"] + lax.axis_index("cells_1")
    ) * sizes["cells_2"] + lax.axis_index("cells_2")


def greet_cells(barrier, sizes, count):
    def one(step, carry):
        peer, _ = cell_peer(step, sizes)
        pl.semaphore_signal(barrier, inc=1, device_id=peer, device_id_type=MESH)
        return carry

    lax.fori_loop(1, count, one, 0)


def start_exchange(sizes, source, target, own_sem, send_sem, recv_sem, part=()):
    count = source.shape[0]
    me = own_cell(sizes)

    def one(step, carry):
        peer, index = cell_peer(step, sizes)
        pltpu.make_async_remote_copy(
            src_ref=source.at[(index, *part)],
            dst_ref=target.at[(me, *part)],
            send_sem=send_sem,
            recv_sem=recv_sem,
            device_id=peer,
            device_id_type=MESH,
        ).start()
        return carry

    lax.fori_loop(1, count, one, 0)
    own = pltpu.make_async_copy(source.at[(me, *part)], target.at[(me, *part)], own_sem)
    own.start()

    def finish():
        others = (pl.ds(0, count - 1), *part)
        pltpu.make_async_copy(source.at[others], target.at[others], recv_sem).wait()
        pltpu.make_async_copy(source.at[others], target.at[others], send_sem).wait()
        own.wait()

    return finish


def placed_part(side, width):
    return (slice(None), pl.ds(side * (width // 2), width // 2))


def column_body(
    sizes, index_ref, parent_ref, noise_ref, out_ref, pairs, columns, own_sem, send_sem, recv_sem
):
    count = pairs.shape[0]
    barrier = pltpu.get_barrier_semaphore()
    greet_cells(barrier, sizes, count)
    pairs[:, 0] = parent_ref[...].astype(pairs.dtype)
    pairs[:, 1] = noise_ref[...].astype(pairs.dtype)
    pl.semaphore_wait(barrier, count - 1)
    start_exchange(sizes, pairs, columns, own_sem, send_sem, recv_sem)()

    def one(k, carry):
        parent = columns[index_ref[k], 0].astype(jnp.float32)
        out_ref[k] = (parent + columns[k, 1].astype(jnp.float32)).astype(out_ref.dtype)
        return carry

    lax.fori_loop(0, count, one, 0)


def child_columns(index, parent, noise, sizes):
    count, *tile = parent.shape
    both = pltpu.VMEM((count, 2, *tile), jnp.bfloat16)
    return pl.pallas_call(
        functools.partial(column_body, sizes),
        out_shape=jax.ShapeDtypeStruct((count, *tile), jnp.bfloat16),
        in_specs=[pl.BlockSpec(memory_space=SMEM)] + [pl.BlockSpec(memory_space=VMEM)] * 2,
        out_specs=pl.BlockSpec(memory_space=VMEM),
        scratch_shapes=[
            both,
            both,
            pltpu.SemaphoreType.DMA(()),
            pltpu.SemaphoreType.DMA(()),
            pltpu.SemaphoreType.DMA(()),
        ],
        compiler_params=pltpu.CompilerParams(collective_id=1, has_side_effects=True),
        name="child_columns",
    )(index, parent, noise)


def prepare_body(weights_ref, act_ref, w_in, mix, wide, w_out):
    half = weights_ref.shape[0] // 2
    wide[...] = weights_ref[:half].reshape(wide.shape).astype(jnp.float32)
    for j in range(HID // LANES):
        w_in[:, j * LANES : (j + 1) * LANES] = wide[
            pl.ds(j, NS, stride=HID // LANES), :
        ].astype(jnp.bfloat16)
    wide[...] = weights_ref[half:].reshape(wide.shape).astype(jnp.float32)
    for j in range(ACT // LANES):
        w_out[:, j * LANES : (j + 1) * LANES] = wide[
            pl.ds(j, HID, stride=ACT // LANES), :
        ].astype(jnp.bfloat16)
    mix[...] = (
        jnp.dot(w_out[...], act_ref[...], preferred_element_type=jnp.float32) * HID ** (-0.5)
    ).astype(jnp.bfloat16)


def prepare(weights, act_map):
    return pl.pallas_call(
        prepare_body,
        out_shape=(
            jax.ShapeDtypeStruct((NS, HID), jnp.bfloat16),
            jax.ShapeDtypeStruct((HID, NS), jnp.bfloat16),
        ),
        in_specs=[pl.BlockSpec(memory_space=VMEM)] * 2,
        out_specs=(pl.BlockSpec(memory_space=VMEM), pl.BlockSpec(memory_space=VMEM)),
        scratch_shapes=[
            pltpu.VMEM((NS * HID // LANES, LANES), jnp.float32),
            pltpu.VMEM((HID, ACT), jnp.bfloat16),
        ],
        name="prepare",
    )(weights, act_map)


def rolled_cost(w_in, mix, start_ref, pushed_ref, dyn_ref, cost_ref):
    envs = start_ref.shape[0]
    side = NS // 2

    def advance(t, carry):
        states, total = carry
        low = states.astype(jnp.bfloat16)
        hidden = jnp.tanh(
            jnp.dot(low, w_in[...], preferred_element_type=jnp.float32) * NS ** (-0.5)
        ).astype(jnp.bfloat16)
        drifted = jnp.concatenate(
            [
                jnp.dot(
                    low[:, n * side : (n + 1) * side],
                    dyn_ref[n],
                    preferred_element_type=jnp.float32,
                )
                for n in range(2)
            ],
            axis=1,
        )
        states = (
            drifted
            + jnp.dot(hidden, mix[...], preferred_element_type=jnp.float32)
            + pushed_ref[t]
        )
        squares = (states * states).reshape(envs // 8, 8, NS)
        return states, total + jnp.sum(squares, axis=0)

    last, total = lax.fori_loop(
        0, STEPS, advance, (start_ref[...], jnp.zeros((8, NS), jnp.float32))
    )
    return jnp.sum(total * cost_ref[...])


def spread_body(
    sizes, columns_ref, placed_ref, out_ref, replaced_ref, own_sem, send_sem, recv_sem
):
    count = sizes["env"]
    me = lax.axis_index("env")
    right, left = lax.rem(me + 1, count), lax.rem(me + count - 1, count)
    cells = columns_ref.shape[0]
    barrier = pltpu.get_barrier_semaphore()
    for peer in (left, right):
        pl.semaphore_signal(barrier, inc=1, device_id={"env": peer}, device_id_type=MESH)
    greet_cells(barrier, sizes, cells)
    pl.semaphore_wait(barrier, cells + 1)
    half = cells // 2
    first, second = pl.ds(0, half), pl.ds(half, half)

    def sent(slot, owner, part, peer):
        copy = pltpu.make_async_remote_copy(
            src_ref=out_ref.at[owner, part],
            dst_ref=out_ref.at[owner, part],
            send_sem=send_sem.at[slot],
            recv_sem=recv_sem.at[slot],
            device_id={"env": peer},
            device_id_type=MESH,
        )
        copy.start()
        return copy

    rows_here = start_exchange(
        sizes, columns_ref, out_ref.at[me], own_sem.at[0], send_sem.at[6], recv_sem.at[6]
    )
    replaced_here = start_exchange(
        sizes,
        placed_ref,
        replaced_ref,
        own_sem.at[1],
        send_sem.at[7],
        recv_sem.at[7],
        placed_part(0, placed_ref.shape[2]),
    )
    rows_here()
    near_right = sent(0, me, first, right)
    near_left = sent(1, me, second, left)
    rest = [sent(2, me, second, right), sent(3, me, first, left)]
    near_right.wait_recv()
    rest.append(sent(4, left, first, right))
    near_left.wait_recv()
    rest.append(sent(5, right, second, left))
    near_right.wait_send()
    near_left.wait_send()
    for copy in rest:
        copy.wait()
    replaced_here()


def spread_children(columns, placed, sizes):
    return pl.pallas_call(
        functools.partial(spread_body, sizes),
        out_shape=(
            jax.ShapeDtypeStruct((sizes["env"], *columns.shape), columns.dtype),
            jax.ShapeDtypeStruct(placed.shape, placed.dtype),
        ),
        in_specs=[pl.BlockSpec(memory_space=VMEM)] * 2,
        out_specs=(pl.BlockSpec(memory_space=VMEM), pl.BlockSpec(memory_space=VMEM)),
        scratch_shapes=[
            pltpu.SemaphoreType.DMA((2,)),
            pltpu.SemaphoreType.DMA((8,)),
            pltpu.SemaphoreType.DMA((8,)),
        ],
        compiler_params=pltpu.CompilerParams(collective_id=2, has_side_effects=True),
        name="spread_children",
    )(columns, placed)


PHASES = (("cells_2", "env"), ("cells_1",), ("cells_0",))


def phase_peers(phase, sizes):
    axes = PHASES[phase]
    offsets = [{}]
    for axis in axes:
        offsets = [{**o, axis: d} for o in offsets for d in range(sizes[axis])]
    peers = []
    for offset in offsets[1:]:
        peers.append(
            {a: lax.rem(lax.axis_index(a) + d, sizes[a]) for a, d in offset.items()}
        )
    return peers


def finish_body(
    sizes,
    w_in,
    mix,
    start_ref,
    pushed_ref,
    dyn_ref,
    cost_ref,
    placed_ref,
    out_ref,
    replaced_ref,
    sums,
    landed,
    own_sem,
    send_sem,
    recv_sem,
    placed_send,
    placed_recv,
):
    everyone = [phase_peers(phase, sizes) for phase in range(len(PHASES))]
    cells = placed_ref.shape[0]
    barrier = pltpu.get_barrier_semaphore()
    greet_cells(barrier, sizes, cells)
    for peer in everyone[0]:
        pl.semaphore_signal(barrier, inc=1, device_id=peer, device_id_type=MESH)
    pl.semaphore_wait(barrier, cells - 1 + len(everyone[0]))
    replaced_here = start_exchange(
        sizes,
        placed_ref,
        replaced_ref,
        own_sem,
        placed_send,
        placed_recv,
        placed_part(1, placed_ref.shape[2]),
    )
    cost = rolled_cost(w_in, mix, start_ref, pushed_ref, dyn_ref, cost_ref)
    lanes = lax.broadcasted_iota(jnp.int32, (8, LANES), 1)
    sums[0] = jnp.where(lanes == own_cell(sizes), cost, 0.0)
    for phase, peers in enumerate(everyone):
        copies = []
        for d, peer in enumerate(peers):
            copy = pltpu.make_async_remote_copy(
                src_ref=sums.at[phase],
                dst_ref=landed.at[phase, d],
                send_sem=send_sem.at[phase, d],
                recv_sem=recv_sem.at[phase, d],
                device_id=peer,
                device_id_type=MESH,
            )
            copy.start()
            copies.append(copy)
        for copy in copies:
            copy.wait()
        total = sums[phase]
        for d in range(len(peers)):
            total = total + landed[phase, d]
        if phase + 1 < len(PHASES):
            sums[phase + 1] = total
        else:
            out_ref[...] = total
    replaced_here()


def roll_and_finish(w_in, mix, start_states, pushed, dyn_pairs, cost_weights, placed, sizes):
    most = 7
    tile = (8, LANES)
    return pl.pallas_call(
        functools.partial(finish_body, sizes),
        out_shape=(
            jax.ShapeDtypeStruct(tile, jnp.float32),
            jax.ShapeDtypeStruct(placed.shape, placed.dtype),
        ),
        in_specs=[pl.BlockSpec(memory_space=VMEM)] * 7,
        out_specs=(pl.BlockSpec(memory_space=VMEM), pl.BlockSpec(memory_space=VMEM)),
        scratch_shapes=[
            pltpu.VMEM((len(PHASES), *tile), jnp.float32),
            pltpu.VMEM((len(PHASES), most, *tile), jnp.float32),
            pltpu.SemaphoreType.DMA(()),
            pltpu.SemaphoreType.DMA((len(PHASES), most)),
            pltpu.SemaphoreType.DMA((len(PHASES), most)),
            pltpu.SemaphoreType.DMA(()),
            pltpu.SemaphoreType.DMA(()),
        ],
        compiler_params=pltpu.CompilerParams(
            collective_id=0, has_side_effects=True, vmem_limit_bytes=40 * 1024 * 1024
        ),
        name="roll_and_finish",
    )(w_in, mix, start_states, pushed, dyn_pairs, cost_weights, placed)


def on_device(
    sizes,
    archive,
    fitness_old,
    parents,
    cell_ids,
    replace_mask,
    noise,
    start_states,
    forces,
    dyn_blocks,
    act_map,
    contact_map,
    cost_weights,
):
    cell_dev = archive.shape[0]
    cell_count = lax.axis_size(CELLS)
    total_cells = cell_dev * cell_count
    offspring_count = parents.shape[0]
    position = lax.axis_index(CELLS)
    tiled = (cell_count, SUB, LANES)

    local_ids = position * cell_dev + jnp.arange(cell_dev, dtype=jnp.int32)
    used_local = jnp.any(parents[None, :] == local_ids[:, None], axis=1)
    compact = jnp.dot(
        used_local[None, :].astype(jnp.bfloat16), archive, preferred_element_type=jnp.float32
    )
    compact = lax.optimization_barrier(compact)
    spread = noise.astype(jnp.float32)
    child_cols = child_columns(
        parents // cell_dev, compact.reshape(tiled), spread.reshape(tiled), sizes
    )

    cell_range = jnp.arange(total_cells, dtype=jnp.int32)
    matches = cell_ids[None, :] == cell_range[:, None]
    eligible = matches & (replace_mask[None, :] == 1)
    indices = jnp.arange(offspring_count, dtype=jnp.int32)
    winner = jnp.max(jnp.where(eligible, indices[None, :], -1), axis=1)
    winning = indices[None, :] == winner[:, None]
    chosen = winner >= 0

    placed = jnp.dot(
        winning.astype(jnp.bfloat16),
        child_cols.reshape(cell_count, SUB * LANES),
        preferred_element_type=jnp.float32,
    ).astype(jnp.bfloat16)
    placed = placed.reshape(cell_count, cell_dev, SUB * LANES)
    weights, left = spread_children(child_cols, placed, sizes)

    envs = start_states.shape[0]
    pushed = jnp.dot(
        forces.reshape(STEPS * envs, -1), contact_map, preferred_element_type=jnp.float32
    ).reshape(STEPS, envs, NS)
    dyn_pairs = (
        dyn_blocks.reshape(2, 2, BLK, 1, BLK)
        * jnp.eye(2, dtype=jnp.bfloat16)[None, :, None, :, None]
    ).reshape(2, 2 * BLK, 2 * BLK)
    w_in, mix = prepare(weights, act_map)
    costs, right = roll_and_finish(
        w_in, mix, start_states, pushed, dyn_pairs, cost_weights.reshape(1, NS), placed, sizes
    )
    all_costs = costs[0]
    in_left = lax.broadcasted_iota(jnp.int32, left.shape, 2) < SUB * LANES // 2
    replaced = jnp.moveaxis(jnp.where(in_left, left, right), 1, 0).reshape(archive.shape)
    own_chosen = lax.dynamic_slice_in_dim(chosen, position * cell_dev, cell_dev, 0)
    new_archive = jnp.where(own_chosen[:, None], replaced, archive)

    envs_total = envs * lax.axis_size("env")
    fitness = -all_costs / (STEPS * envs_total * NS)
    own_winning = lax.dynamic_slice_in_dim(winning, position * cell_dev, cell_dev, 0)
    own_matches = lax.dynamic_slice_in_dim(matches, position * cell_dev, cell_dev, 0)
    winner_fitness = jnp.sum(jnp.where(own_winning, fitness[None, :], 0.0), axis=1)
    new_fitness = jnp.where(own_chosen, winner_fitness, fitness_old)
    lifted = jnp.maximum(fitness[None, :] - fitness_old[:, None], 0.0)
    cell_gain = jnp.sum(jnp.where(own_matches, lifted, 0.0), axis=1)
    return (new_archive, new_fitness, cell_gain)


def solution(mesh):
    split = Mesh(
        mesh.devices.reshape(8, 8, 2, mesh.shape["env"]), ("cells_0", "cells_1", "cells_2", "env")
    )
    return jax.shard_map(
        functools.partial(on_device, dict(split.shape)),
        mesh=split,
        in_specs=(
            P(CELLS, "env"),
            P(CELLS),
            P(),
            P(),
            P(),
            P(CELLS, "env"),
            P("env", None),
            P(None, "env", None),
            P(),
            P(),
            P(),
            P(),
        ),
        out_specs=(P(CELLS, "env"), P(CELLS), P(CELLS)),
        check_vma=False,
    )
```

```python
import functools

import jax
import jax.numpy as jnp
from jax import lax
from jax.experimental import pallas as pl
from jax.experimental.pallas import tpu as pltpu
from jax.sharding import Mesh
from jax.sharding import PartitionSpec as P

NS = 512
HID = 1024
ACT = 512
BLK = 128
STEPS = 16
CELLS = ("cells_0", "cells_1", "cells_2")
LANES = 128
SUB = 16
LEFT_QUARTERS = 3
VMEM = pltpu.MemorySpace.VMEM
SMEM = pltpu.MemorySpace.SMEM


MESH = pl.DeviceIdType.MESH


def cell_peer(step, sizes):
    rows, columns, cores = (sizes[a] for a in CELLS)
    mixed = lax.rem(step * 37, rows * columns * cores)
    row = lax.rem(lax.axis_index("cells_0") + lax.div(mixed, columns * cores), rows)
    column = lax.rem(
        lax.axis_index("cells_1") + lax.rem(lax.div(mixed, cores), columns), columns
    )
    core = lax.rem(lax.axis_index("cells_2") + lax.rem(mixed, cores), cores)
    peer = {"cells_0": row, "cells_1": column, "cells_2": core}
    return peer, (row * columns + column) * cores + core


def own_cell(sizes):
    return (
        lax.axis_index("cells_0") * sizes["cells_1"] + lax.axis_index("cells_1")
    ) * sizes["cells_2"] + lax.axis_index("cells_2")


def greet_cells(barrier, sizes, count):
    def one(step, carry):
        peer, _ = cell_peer(step, sizes)
        pl.semaphore_signal(barrier, inc=1, device_id=peer, device_id_type=MESH)
        return carry

    lax.fori_loop(1, count, one, 0)


def start_exchange(sizes, source, target, own_sem, send_sem, recv_sem, part=()):
    count = source.shape[0]
    me = own_cell(sizes)

    def one(step, carry):
        peer, index = cell_peer(step, sizes)
        pltpu.make_async_remote_copy(
            src_ref=source.at[(index, *part)],
            dst_ref=target.at[(me, *part)],
            send_sem=send_sem,
            recv_sem=recv_sem,
            device_id=peer,
            device_id_type=MESH,
        ).start()
        return carry

    lax.fori_loop(1, count, one, 0)
    own = pltpu.make_async_copy(source.at[(me, *part)], target.at[(me, *part)], own_sem)
    own.start()

    def finish():
        others = (pl.ds(0, count - 1), *part)
        pltpu.make_async_copy(source.at[others], target.at[others], recv_sem).wait()
        pltpu.make_async_copy(source.at[others], target.at[others], send_sem).wait()
        own.wait()

    return finish


def placed_part(side, width):
    edge = LEFT_QUARTERS * (width // 4)
    return (slice(None), pl.ds(0, edge) if side == 0 else pl.ds(edge, width - edge))


def column_body(
    sizes, index_ref, parent_ref, noise_ref, out_ref, pairs, columns, own_sem, send_sem, recv_sem
):
    count = pairs.shape[0]
    barrier = pltpu.get_barrier_semaphore()
    greet_cells(barrier, sizes, count)
    pairs[:, 0] = parent_ref[...].astype(pairs.dtype)
    pairs[:, 1] = noise_ref[...].astype(pairs.dtype)
    pl.semaphore_wait(barrier, count - 1)
    start_exchange(sizes, pairs, columns, own_sem, send_sem, recv_sem)()

    def one(k, carry):
        parent = columns[index_ref[k], 0].astype(jnp.float32)
        out_ref[k] = (parent + columns[k, 1].astype(jnp.float32)).astype(out_ref.dtype)
        return carry

    lax.fori_loop(0, count, one, 0)


def child_columns(index, parent, noise, sizes):
    count, *tile = parent.shape
    both = pltpu.VMEM((count, 2, *tile), jnp.bfloat16)
    return pl.pallas_call(
        functools.partial(column_body, sizes),
        out_shape=jax.ShapeDtypeStruct((count, *tile), jnp.bfloat16),
        in_specs=[pl.BlockSpec(memory_space=SMEM)] + [pl.BlockSpec(memory_space=VMEM)] * 2,
        out_specs=pl.BlockSpec(memory_space=VMEM),
        scratch_shapes=[
            both,
            both,
            pltpu.SemaphoreType.DMA(()),
            pltpu.SemaphoreType.DMA(()),
            pltpu.SemaphoreType.DMA(()),
        ],
        compiler_params=pltpu.CompilerParams(collective_id=1, has_side_effects=True),
        name="child_columns",
    )(index, parent, noise)


def prepare_body(weights_ref, act_ref, w_in, mix, wide, w_out):
    half = weights_ref.shape[0] // 2
    wide[...] = weights_ref[:half].reshape(wide.shape).astype(jnp.float32)
    for j in range(HID // LANES):
        w_in[:, j * LANES : (j + 1) * LANES] = wide[
            pl.ds(j, NS, stride=HID // LANES), :
        ].astype(jnp.bfloat16)
    wide[...] = weights_ref[half:].reshape(wide.shape).astype(jnp.float32)
    for j in range(ACT // LANES):
        w_out[:, j * LANES : (j + 1) * LANES] = wide[
            pl.ds(j, HID, stride=ACT // LANES), :
        ].astype(jnp.bfloat16)
    mix[...] = (
        jnp.dot(w_out[...], act_ref[...], preferred_element_type=jnp.float32) * HID ** (-0.5)
    ).astype(jnp.bfloat16)


def prepare(weights, act_map):
    return pl.pallas_call(
        prepare_body,
        out_shape=(
            jax.ShapeDtypeStruct((NS, HID), jnp.bfloat16),
            jax.ShapeDtypeStruct((HID, NS), jnp.bfloat16),
        ),
        in_specs=[pl.BlockSpec(memory_space=VMEM)] * 2,
        out_specs=(pl.BlockSpec(memory_space=VMEM), pl.BlockSpec(memory_space=VMEM)),
        scratch_shapes=[
            pltpu.VMEM((NS * HID // LANES, LANES), jnp.float32),
            pltpu.VMEM((HID, ACT), jnp.bfloat16),
        ],
        name="prepare",
    )(weights, act_map)


def rolled_cost(w_in, mix, start_ref, pushed_ref, dyn_ref, cost_ref, midway):
    envs = start_ref.shape[0]

    def advance(t, carry):
        states, total = carry
        low = states.astype(jnp.bfloat16)
        hidden = jnp.tanh(
            jnp.dot(low, w_in[...], preferred_element_type=jnp.float32) * NS ** (-0.5)
        ).astype(jnp.bfloat16)
        drifted = jnp.concatenate(
            [
                jnp.dot(
                    low[:, n * BLK : (n + 1) * BLK],
                    dyn_ref[n],
                    preferred_element_type=jnp.float32,
                )
                for n in range(NS // BLK)
            ],
            axis=1,
        )
        states = (
            drifted
            + jnp.dot(hidden, mix[...], preferred_element_type=jnp.float32)
            + pushed_ref[t]
        )
        squares = (states * states).reshape(envs // 8, 8, NS)
        return states, total + jnp.sum(squares, axis=0)

    carry = (start_ref[...], jnp.zeros((8, NS), jnp.float32))
    carry = lax.fori_loop(0, STEPS // 2, advance, carry)
    left_over = midway()
    last, total = lax.fori_loop(STEPS // 2, STEPS, advance, carry)
    return jnp.sum(total * cost_ref[...]), left_over


def spread_body(
    sizes, columns_ref, placed_ref, out_ref, replaced_ref, own_sem, send_sem, recv_sem
):
    count = sizes["env"]
    me = lax.axis_index("env")
    right, left = lax.rem(me + 1, count), lax.rem(me + count - 1, count)
    cells = columns_ref.shape[0]
    barrier = pltpu.get_barrier_semaphore()
    for peer in (left, right):
        pl.semaphore_signal(barrier, inc=1, device_id={"env": peer}, device_id_type=MESH)
    greet_cells(barrier, sizes, cells)
    pl.semaphore_wait(barrier, cells + 1)
    half = cells // 2
    first, second = pl.ds(0, half), pl.ds(half, half)

    def sent(slot, owner, part, peer):
        copy = pltpu.make_async_remote_copy(
            src_ref=out_ref.at[owner, part],
            dst_ref=out_ref.at[owner, part],
            send_sem=send_sem.at[slot],
            recv_sem=recv_sem.at[slot],
            device_id={"env": peer},
            device_id_type=MESH,
        )
        copy.start()
        return copy

    rows_here = start_exchange(
        sizes, columns_ref, out_ref.at[me], own_sem.at[0], send_sem.at[6], recv_sem.at[6]
    )
    rows_here()
    near_right = sent(0, me, first, right)
    near_left = sent(1, me, second, left)
    rest = [sent(2, me, second, right), sent(3, me, first, left)]
    replaced_here = start_exchange(
        sizes,
        placed_ref,
        replaced_ref,
        own_sem.at[1],
        send_sem.at[7],
        recv_sem.at[7],
        placed_part(0, placed_ref.shape[2]),
    )
    near_right.wait_recv()
    rest.append(sent(4, left, first, right))
    near_left.wait_recv()
    rest.append(sent(5, right, second, left))
    near_right.wait_send()
    near_left.wait_send()
    for copy in rest:
        copy.wait()
    replaced_here()


def spread_children(columns, placed, sizes):
    return pl.pallas_call(
        functools.partial(spread_body, sizes),
        out_shape=(
            jax.ShapeDtypeStruct((sizes["env"], *columns.shape), columns.dtype),
            jax.ShapeDtypeStruct(placed.shape, placed.dtype),
        ),
        in_specs=[pl.BlockSpec(memory_space=VMEM)] * 2,
        out_specs=(pl.BlockSpec(memory_space=VMEM), pl.BlockSpec(memory_space=VMEM)),
        scratch_shapes=[
            pltpu.SemaphoreType.DMA((2,)),
            pltpu.SemaphoreType.DMA((8,)),
            pltpu.SemaphoreType.DMA((8,)),
        ],
        compiler_params=pltpu.CompilerParams(collective_id=2, has_side_effects=True),
        name="spread_children",
    )(columns, placed)


PHASES = (("cells_2", "env"), ("cells_1",), ("cells_0",))


def phase_peers(phase, sizes):
    axes = PHASES[phase]
    offsets = [{}]
    for axis in axes:
        offsets = [{**o, axis: d} for o in offsets for d in range(sizes[axis])]
    peers = []
    for offset in offsets[1:]:
        peers.append(
            {a: lax.rem(lax.axis_index(a) + d, sizes[a]) for a, d in offset.items()}
        )
    return peers


def finish_body(
    sizes,
    w_in,
    mix,
    start_ref,
    pushed_ref,
    dyn_ref,
    cost_ref,
    placed_ref,
    out_ref,
    replaced_ref,
    sums,
    landed,
    own_sem,
    send_sem,
    recv_sem,
    placed_send,
    placed_recv,
):
    everyone = [phase_peers(phase, sizes) for phase in range(len(PHASES))]
    cells = placed_ref.shape[0]
    barrier = pltpu.get_barrier_semaphore()
    greet_cells(barrier, sizes, cells)
    for peer in everyone[0]:
        pl.semaphore_signal(barrier, inc=1, device_id=peer, device_id_type=MESH)

    def midway():
        pl.semaphore_wait(barrier, cells - 1 + len(everyone[0]))
        return start_exchange(
            sizes,
            placed_ref,
            replaced_ref,
            own_sem,
            placed_send,
            placed_recv,
            placed_part(1, placed_ref.shape[2]),
        )

    cost, replaced_here = rolled_cost(
        w_in, mix, start_ref, pushed_ref, dyn_ref, cost_ref, midway
    )
    lanes = lax.broadcasted_iota(jnp.int32, (8, LANES), 1)
    sums[0] = jnp.where(lanes == own_cell(sizes), cost, 0.0)
    for phase, peers in enumerate(everyone):
        copies = []
        for d, peer in enumerate(peers):
            copy = pltpu.make_async_remote_copy(
                src_ref=sums.at[phase],
                dst_ref=landed.at[phase, d],
                send_sem=send_sem.at[phase, d],
                recv_sem=recv_sem.at[phase, d],
                device_id=peer,
                device_id_type=MESH,
            )
            copy.start()
            copies.append(copy)
        for copy in copies:
            copy.wait()
        total = sums[phase]
        for d in range(len(peers)):
            total = total + landed[phase, d]
        if phase + 1 < len(PHASES):
            sums[phase + 1] = total
        else:
            out_ref[...] = total
    replaced_here()


def roll_and_finish(w_in, mix, start_states, pushed, dyn_blocks, cost_weights, placed, sizes):
    most = 7
    tile = (8, LANES)
    return pl.pallas_call(
        functools.partial(finish_body, sizes),
        out_shape=(
            jax.ShapeDtypeStruct(tile, jnp.float32),
            jax.ShapeDtypeStruct(placed.shape, placed.dtype),
        ),
        in_specs=[pl.BlockSpec(memory_space=VMEM)] * 7,
        out_specs=(pl.BlockSpec(memory_space=VMEM), pl.BlockSpec(memory_space=VMEM)),
        scratch_shapes=[
            pltpu.VMEM((len(PHASES), *tile), jnp.float32),
            pltpu.VMEM((len(PHASES), most, *tile), jnp.float32),
            pltpu.SemaphoreType.DMA(()),
            pltpu.SemaphoreType.DMA((len(PHASES), most)),
            pltpu.SemaphoreType.DMA((len(PHASES), most)),
            pltpu.SemaphoreType.DMA(()),
            pltpu.SemaphoreType.DMA(()),
        ],
        compiler_params=pltpu.CompilerParams(
            collective_id=0, has_side_effects=True, vmem_limit_bytes=40 * 1024 * 1024
        ),
        name="roll_and_finish",
    )(w_in, mix, start_states, pushed, dyn_blocks, cost_weights, placed)


def on_device(
    sizes,
    archive,
    fitness_old,
    parents,
    cell_ids,
    replace_mask,
    noise,
    start_states,
    forces,
    dyn_blocks,
    act_map,
    contact_map,
    cost_weights,
):
    cell_dev = archive.shape[0]
    cell_count = lax.axis_size(CELLS)
    total_cells = cell_dev * cell_count
    offspring_count = parents.shape[0]
    position = lax.axis_index(CELLS)
    tiled = (cell_count, SUB, LANES)

    local_ids = position * cell_dev + jnp.arange(cell_dev, dtype=jnp.int32)
    used_local = jnp.any(parents[None, :] == local_ids[:, None], axis=1)
    compact = jnp.dot(
        used_local[None, :].astype(jnp.bfloat16), archive, preferred_element_type=jnp.float32
    )
    compact = lax.optimization_barrier(compact)
    spread = noise.astype(jnp.float32)
    child_cols = child_columns(
        parents // cell_dev, compact.reshape(tiled), spread.reshape(tiled), sizes
    )

    cell_range = jnp.arange(total_cells, dtype=jnp.int32)
    matches = cell_ids[None, :] == cell_range[:, None]
    eligible = matches & (replace_mask[None, :] == 1)
    indices = jnp.arange(offspring_count, dtype=jnp.int32)
    winner = jnp.max(jnp.where(eligible, indices[None, :], -1), axis=1)
    winning = indices[None, :] == winner[:, None]
    chosen = winner >= 0

    placed = jnp.dot(
        winning.astype(jnp.bfloat16),
        child_cols.reshape(cell_count, SUB * LANES),
        preferred_element_type=jnp.float32,
    ).astype(jnp.bfloat16)
    placed = placed.reshape(cell_count, cell_dev, SUB * LANES)
    weights, left = spread_children(child_cols, placed, sizes)

    envs = start_states.shape[0]
    pushed = jnp.dot(
        forces.reshape(STEPS * envs, -1), contact_map, preferred_element_type=jnp.float32
    ).reshape(STEPS, envs, NS)
    w_in, mix = prepare(weights, act_map)
    costs, right = roll_and_finish(
        w_in, mix, start_states, pushed, dyn_blocks, cost_weights.reshape(1, NS), placed, sizes
    )
    all_costs = costs[0]
    in_left = lax.broadcasted_iota(jnp.int32, left.shape, 2) < LEFT_QUARTERS * SUB * LANES // 4
    replaced = jnp.moveaxis(jnp.where(in_left, left, right), 1, 0).reshape(archive.shape)
    own_chosen = lax.dynamic_slice_in_dim(chosen, position * cell_dev, cell_dev, 0)
    new_archive = jnp.where(own_chosen[:, None], replaced, archive)

    envs_total = envs * lax.axis_size("env")
    fitness = -all_costs / (STEPS * envs_total * NS)
    own_winning = lax.dynamic_slice_in_dim(winning, position * cell_dev, cell_dev, 0)
    own_matches = lax.dynamic_slice_in_dim(matches, position * cell_dev, cell_dev, 0)
    winner_fitness = jnp.sum(jnp.where(own_winning, fitness[None, :], 0.0), axis=1)
    new_fitness = jnp.where(own_chosen, winner_fitness, fitness_old)
    lifted = jnp.maximum(fitness[None, :] - fitness_old[:, None], 0.0)
    cell_gain = jnp.sum(jnp.where(own_matches, lifted, 0.0), axis=1)
    return (new_archive, new_fitness, cell_gain)


def solution(mesh):
    split = Mesh(
        mesh.devices.reshape(8, 8, 2, mesh.shape["env"]), ("cells_0", "cells_1", "cells_2", "env")
    )
    return jax.shard_map(
        functools.partial(on_device, dict(split.shape)),
        mesh=split,
        in_specs=(
            P(CELLS, "env"),
            P(CELLS),
            P(),
            P(),
            P(),
            P(CELLS, "env"),
            P("env", None),
            P(None, "env", None),
            P(),
            P(),
            P(),
            P(),
        ),
        out_specs=(P(CELLS, "env"), P(CELLS), P(CELLS)),
        check_vma=False,
    )
```

```python
import functools

import jax
import jax.numpy as jnp
from jax import lax
from jax.experimental import pallas as pl
from jax.experimental.pallas import tpu as pltpu
from jax.sharding import Mesh
from jax.sharding import PartitionSpec as P

NS = 512
HID = 1024
ACT = 512
BLK = 128
STEPS = 16
CELLS = ("cells_0", "cells_1", "cells_2")
LANES = 128
SUB = 16
VMEM = pltpu.MemorySpace.VMEM
SMEM = pltpu.MemorySpace.SMEM


MESH = pl.DeviceIdType.MESH


def cell_peer(step, sizes):
    rows, columns, cores = (sizes[a] for a in CELLS)
    mixed = lax.rem(step * 37, rows * columns * cores)
    row = lax.rem(lax.axis_index("cells_0") + lax.div(mixed, columns * cores), rows)
    column = lax.rem(
        lax.axis_index("cells_1") + lax.rem(lax.div(mixed, cores), columns), columns
    )
    core = lax.rem(lax.axis_index("cells_2") + lax.rem(mixed, cores), cores)
    peer = {"cells_0": row, "cells_1": column, "cells_2": core}
    return peer, (row * columns + column) * cores + core


def own_cell(sizes):
    return (
        lax.axis_index("cells_0") * sizes["cells_1"] + lax.axis_index("cells_1")
    ) * sizes["cells_2"] + lax.axis_index("cells_2")


def greet_cells(barrier, sizes, count):
    def one(step, carry):
        peer, _ = cell_peer(step, sizes)
        pl.semaphore_signal(barrier, inc=1, device_id=peer, device_id_type=MESH)
        return carry

    lax.fori_loop(1, count, one, 0)


def start_exchange(sizes, source, target, own_sem, send_sem, recv_sem):
    count = source.shape[0]
    me = own_cell(sizes)

    def one(step, carry):
        peer, index = cell_peer(step, sizes)
        pltpu.make_async_remote_copy(
            src_ref=source.at[index],
            dst_ref=target.at[me],
            send_sem=send_sem,
            recv_sem=recv_sem,
            device_id=peer,
            device_id_type=MESH,
        ).start()
        return carry

    lax.fori_loop(1, count, one, 0)
    own = pltpu.make_async_copy(source.at[me], target.at[me], own_sem)
    own.start()

    def finish():
        others = pl.ds(0, count - 1)
        pltpu.make_async_copy(source.at[others], target.at[others], recv_sem).wait()
        pltpu.make_async_copy(source.at[others], target.at[others], send_sem).wait()
        own.wait()

    return finish


def column_body(
    sizes, index_ref, parent_ref, noise_ref, out_ref, pairs, columns, own_sem, send_sem, recv_sem
):
    count = pairs.shape[0]
    barrier = pltpu.get_barrier_semaphore()
    greet_cells(barrier, sizes, count)
    pairs[:, 0] = parent_ref[...].astype(pairs.dtype)
    pairs[:, 1] = noise_ref[...].astype(pairs.dtype)
    pl.semaphore_wait(barrier, count - 1)
    start_exchange(sizes, pairs, columns, own_sem, send_sem, recv_sem)()

    def one(k, carry):
        parent = columns[index_ref[k], 0].astype(jnp.float32)
        out_ref[k] = (parent + columns[k, 1].astype(jnp.float32)).astype(out_ref.dtype)
        return carry

    lax.fori_loop(0, count, one, 0)


def child_columns(index, parent, noise, sizes):
    count, *tile = parent.shape
    both = pltpu.VMEM((count, 2, *tile), jnp.bfloat16)
    return pl.pallas_call(
        functools.partial(column_body, sizes),
        out_shape=jax.ShapeDtypeStruct((count, *tile), jnp.bfloat16),
        in_specs=[pl.BlockSpec(memory_space=SMEM)] + [pl.BlockSpec(memory_space=VMEM)] * 2,
        out_specs=pl.BlockSpec(memory_space=VMEM),
        scratch_shapes=[
            both,
            both,
            pltpu.SemaphoreType.DMA(()),
            pltpu.SemaphoreType.DMA(()),
            pltpu.SemaphoreType.DMA(()),
        ],
        compiler_params=pltpu.CompilerParams(collective_id=1, has_side_effects=True),
        name="child_columns",
    )(index, parent, noise)


def prepare_body(weights_ref, act_ref, w_in, mix, wide, w_out):
    half = weights_ref.shape[0] // 2
    wide[...] = weights_ref[:half].reshape(wide.shape).astype(jnp.float32)
    for j in range(HID // LANES):
        w_in[:, j * LANES : (j + 1) * LANES] = wide[
            pl.ds(j, NS, stride=HID // LANES), :
        ].astype(jnp.bfloat16)
    wide[...] = weights_ref[half:].reshape(wide.shape).astype(jnp.float32)
    for j in range(ACT // LANES):
        w_out[:, j * LANES : (j + 1) * LANES] = wide[
            pl.ds(j, HID, stride=ACT // LANES), :
        ].astype(jnp.bfloat16)
    mix[...] = (
        jnp.dot(w_out[...], act_ref[...], preferred_element_type=jnp.float32) * HID ** (-0.5)
    ).astype(jnp.bfloat16)


def prepare(weights, act_map):
    return pl.pallas_call(
        prepare_body,
        out_shape=(
            jax.ShapeDtypeStruct((NS, HID), jnp.bfloat16),
            jax.ShapeDtypeStruct((HID, NS), jnp.bfloat16),
        ),
        in_specs=[pl.BlockSpec(memory_space=VMEM)] * 2,
        out_specs=(pl.BlockSpec(memory_space=VMEM), pl.BlockSpec(memory_space=VMEM)),
        scratch_shapes=[
            pltpu.VMEM((NS * HID // LANES, LANES), jnp.float32),
            pltpu.VMEM((HID, ACT), jnp.bfloat16),
        ],
        name="prepare",
    )(weights, act_map)


def rolled_cost(w_in, mix, start_ref, pushed_ref, dyn_ref, cost_ref):
    envs = start_ref.shape[0]

    def advance(t, carry):
        states, total = carry
        low = states.astype(jnp.bfloat16)
        hidden = jnp.tanh(
            jnp.dot(low, w_in[...], preferred_element_type=jnp.float32) * NS ** (-0.5)
        ).astype(jnp.bfloat16)
        drifted = jnp.concatenate(
            [
                jnp.dot(
                    low[:, n * BLK : (n + 1) * BLK],
                    dyn_ref[n],
                    preferred_element_type=jnp.float32,
                )
                for n in range(NS // BLK)
            ],
            axis=1,
        )
        states = (
            drifted
            + jnp.dot(hidden, mix[...], preferred_element_type=jnp.float32)
            + pushed_ref[t]
        )
        squares = (states * states).reshape(envs // 8, 8, NS)
        return states, total + jnp.sum(squares, axis=0)

    last, total = lax.fori_loop(
        0, STEPS, advance, (start_ref[...], jnp.zeros((8, NS), jnp.float32))
    )
    return jnp.sum(total * cost_ref[...])


def spread_body(
    sizes, columns_ref, placed_ref, out_ref, replaced_ref, own_sem, send_sem, recv_sem
):
    count = sizes["env"]
    me = lax.axis_index("env")
    right, left = lax.rem(me + 1, count), lax.rem(me + count - 1, count)
    cells = columns_ref.shape[0]
    barrier = pltpu.get_barrier_semaphore()
    for peer in (left, right):
        pl.semaphore_signal(barrier, inc=1, device_id={"env": peer}, device_id_type=MESH)
    greet_cells(barrier, sizes, cells)
    pl.semaphore_wait(barrier, cells + 1)
    half = cells // 2
    first, second = pl.ds(0, half), pl.ds(half, half)

    def sent(slot, owner, part, peer):
        copy = pltpu.make_async_remote_copy(
            src_ref=out_ref.at[owner, part],
            dst_ref=out_ref.at[owner, part],
            send_sem=send_sem.at[slot],
            recv_sem=recv_sem.at[slot],
            device_id={"env": peer},
            device_id_type=MESH,
        )
        copy.start()
        return copy

    rows_here = start_exchange(
        sizes, columns_ref, out_ref.at[me], own_sem.at[0], send_sem.at[6], recv_sem.at[6]
    )
    replaced_here = start_exchange(
        sizes, placed_ref, replaced_ref, own_sem.at[1], send_sem.at[7], recv_sem.at[7]
    )
    rows_here()
    near_right = sent(0, me, first, right)
    near_left = sent(1, me, second, left)
    rest = [sent(2, me, second, right), sent(3, me, first, left)]
    near_right.wait_recv()
    rest.append(sent(4, left, first, right))
    near_left.wait_recv()
    rest.append(sent(5, right, second, left))
    near_right.wait_send()
    near_left.wait_send()
    for copy in rest:
        copy.wait()
    replaced_here()


def spread_children(columns, placed, sizes):
    return pl.pallas_call(
        functools.partial(spread_body, sizes),
        out_shape=(
            jax.ShapeDtypeStruct((sizes["env"], *columns.shape), columns.dtype),
            jax.ShapeDtypeStruct(placed.shape, placed.dtype),
        ),
        in_specs=[pl.BlockSpec(memory_space=VMEM)] * 2,
        out_specs=(pl.BlockSpec(memory_space=VMEM), pl.BlockSpec(memory_space=VMEM)),
        scratch_shapes=[
            pltpu.SemaphoreType.DMA((2,)),
            pltpu.SemaphoreType.DMA((8,)),
            pltpu.SemaphoreType.DMA((8,)),
        ],
        compiler_params=pltpu.CompilerParams(collective_id=2, has_side_effects=True),
        name="spread_children",
    )(columns, placed)


PHASES = (("cells_2", "env"), ("cells_1",), ("cells_0",))


def phase_peers(phase, sizes):
    axes = PHASES[phase]
    offsets = [{}]
    for axis in axes:
        offsets = [{**o, axis: d} for o in offsets for d in range(sizes[axis])]
    peers = []
    for offset in offsets[1:]:
        peers.append(
            {a: lax.rem(lax.axis_index(a) + d, sizes[a]) for a, d in offset.items()}
        )
    return peers


def finish_body(
    sizes,
    w_in,
    mix,
    start_ref,
    pushed_ref,
    dyn_ref,
    cost_ref,
    out_ref,
    sums,
    landed,
    send_sem,
    recv_sem,
):
    everyone = [phase_peers(phase, sizes) for phase in range(len(PHASES))]
    barrier = pltpu.get_barrier_semaphore()
    for peers in everyone:
        for peer in peers:
            pl.semaphore_signal(barrier, inc=1, device_id=peer, device_id_type=MESH)
    cost = rolled_cost(w_in, mix, start_ref, pushed_ref, dyn_ref, cost_ref)
    lanes = lax.broadcasted_iota(jnp.int32, (8, LANES), 1)
    sums[0] = jnp.where(lanes == own_cell(sizes), cost, 0.0)
    pl.semaphore_wait(barrier, sum(len(peers) for peers in everyone))
    for phase, peers in enumerate(everyone):
        copies = []
        for d, peer in enumerate(peers):
            copy = pltpu.make_async_remote_copy(
                src_ref=sums.at[phase],
                dst_ref=landed.at[phase, d],
                send_sem=send_sem.at[phase, d],
                recv_sem=recv_sem.at[phase, d],
                device_id=peer,
                device_id_type=MESH,
            )
            copy.start()
            copies.append(copy)
        for copy in copies:
            copy.wait()
        total = sums[phase]
        for d in range(len(peers)):
            total = total + landed[phase, d]
        if phase + 1 < len(PHASES):
            sums[phase + 1] = total
        else:
            out_ref[...] = total


def roll_and_sum(w_in, mix, start_states, pushed, dyn_blocks, cost_weights, sizes):
    most = 7
    tile = (8, LANES)
    return pl.pallas_call(
        functools.partial(finish_body, sizes),
        out_shape=jax.ShapeDtypeStruct(tile, jnp.float32),
        in_specs=[pl.BlockSpec(memory_space=VMEM)] * 6,
        out_specs=pl.BlockSpec(memory_space=VMEM),
        scratch_shapes=[
            pltpu.VMEM((len(PHASES), *tile), jnp.float32),
            pltpu.VMEM((len(PHASES), most, *tile), jnp.float32),
            pltpu.SemaphoreType.DMA((len(PHASES), most)),
            pltpu.SemaphoreType.DMA((len(PHASES), most)),
        ],
        compiler_params=pltpu.CompilerParams(
            collective_id=0, has_side_effects=True, vmem_limit_bytes=40 * 1024 * 1024
        ),
        name="roll_and_sum",
    )(w_in, mix, start_states, pushed, dyn_blocks, cost_weights)


def on_device(
    sizes,
    archive,
    fitness_old,
    parents,
    cell_ids,
    replace_mask,
    noise,
    start_states,
    forces,
    dyn_blocks,
    act_map,
    contact_map,
    cost_weights,
):
    cell_dev = archive.shape[0]
    cell_count = lax.axis_size(CELLS)
    total_cells = cell_dev * cell_count
    offspring_count = parents.shape[0]
    position = lax.axis_index(CELLS)
    tiled = (cell_count, SUB, LANES)

    local_ids = position * cell_dev + jnp.arange(cell_dev, dtype=jnp.int32)
    used_local = jnp.any(parents[None, :] == local_ids[:, None], axis=1)
    compact = jnp.dot(
        used_local[None, :].astype(jnp.bfloat16), archive, preferred_element_type=jnp.float32
    )
    compact = lax.optimization_barrier(compact)
    spread = noise.astype(jnp.float32)
    child_cols = child_columns(
        parents // cell_dev, compact.reshape(tiled), spread.reshape(tiled), sizes
    )

    cell_range = jnp.arange(total_cells, dtype=jnp.int32)
    matches = cell_ids[None, :] == cell_range[:, None]
    eligible = matches & (replace_mask[None, :] == 1)
    indices = jnp.arange(offspring_count, dtype=jnp.int32)
    winner = jnp.max(jnp.where(eligible, indices[None, :], -1), axis=1)
    winning = indices[None, :] == winner[:, None]
    chosen = winner >= 0

    placed = jnp.dot(
        winning.astype(jnp.bfloat16),
        child_cols.reshape(cell_count, SUB * LANES),
        preferred_element_type=jnp.float32,
    ).astype(jnp.bfloat16)
    placed = placed.reshape(cell_count, cell_dev, SUB * LANES)
    weights, replaced = spread_children(child_cols, placed, sizes)

    envs = start_states.shape[0]
    pushed = jnp.dot(
        forces.reshape(STEPS * envs, -1), contact_map, preferred_element_type=jnp.float32
    ).reshape(STEPS, envs, NS)
    w_in, mix = prepare(weights, act_map)
    all_costs = roll_and_sum(
        w_in, mix, start_states, pushed, dyn_blocks, cost_weights.reshape(1, NS), sizes
    )[0]
    replaced = jnp.moveaxis(replaced, 1, 0).reshape(archive.shape)
    own_chosen = lax.dynamic_slice_in_dim(chosen, position * cell_dev, cell_dev, 0)
    new_archive = jnp.where(own_chosen[:, None], replaced, archive)

    envs_total = envs * lax.axis_size("env")
    fitness = -all_costs / (STEPS * envs_total * NS)
    own_winning = lax.dynamic_slice_in_dim(winning, position * cell_dev, cell_dev, 0)
    own_matches = lax.dynamic_slice_in_dim(matches, position * cell_dev, cell_dev, 0)
    winner_fitness = jnp.sum(jnp.where(own_winning, fitness[None, :], 0.0), axis=1)
    new_fitness = jnp.where(own_chosen, winner_fitness, fitness_old)
    lifted = jnp.maximum(fitness[None, :] - fitness_old[:, None], 0.0)
    cell_gain = jnp.sum(jnp.where(own_matches, lifted, 0.0), axis=1)
    return (new_archive, new_fitness, cell_gain)


def solution(mesh):
    split = Mesh(
        mesh.devices.reshape(8, 8, 2, mesh.shape["env"]), ("cells_0", "cells_1", "cells_2", "env")
    )
    return jax.shard_map(
        functools.partial(on_device, dict(split.shape)),
        mesh=split,
        in_specs=(
            P(CELLS, "env"),
            P(CELLS),
            P(),
            P(),
            P(),
            P(CELLS, "env"),
            P("env", None),
            P(None, "env", None),
            P(),
            P(),
            P(),
            P(),
        ),
        out_specs=(P(CELLS, "env"), P(CELLS), P(CELLS)),
        check_vma=False,
    )
```
